512 devices in a mesh: section: 16 (over x, z_hi), tensor: 32 (over y, z_lo, core).
Axes of the slice: x: 4, y: 8, z: 8 (z_hi: 4, z_lo: 2; z = z_hi * 2 + z_lo), core: 2. Of those that a mesh axis runs over, the one named last changes fastest.
Arguments:
- x_in: bfloat16 [16, 512, 4096], P('section', 'tensor'), may hold values from -40 to 40
- grad_out: bfloat16 [16, 512, 4096], P('section', 'tensor'), may hold values from -50 to 50
- gain: float32 [16, 4096], P('section'), may hold values from 0.5 to 1.5
- w_val: bfloat16 [16, 4096, 4096], P('section', 'tensor'), may hold values from -0.09375 to 0.09375
- w_out: bfloat16 [16, 4096, 4096], P('section', 'tensor'), may hold values from -0.09375 to 0.09375
- filt: float32 [16, 3, 4096], P('section', None, 'tensor'), may hold values from -3 to 3
- tail: bfloat16 [16, 2, 4096], P('section', None, 'tensor'), may hold values from -6 to 6
- micro_index: int32 [16], P('section'), may hold values from 0 to 15
Outputs:
- grad_in: bfloat16 [16, 512, 4096], P('section', 'tensor')
- grad_w_val: bfloat16 [16, 4096, 4096], P('section', 'tensor')
- grad_w_out: bfloat16 [16, 4096, 4096], P('section', 'tensor')
- grad_filter: float32 [16, 3, 4096], P('section', None, 'tensor')
- grad_tail: float32 [16, 2, 4096], P('section', None, 'tensor')
- grad_gain: float32 [16, 4096], P('section')
The draws below stay inside these ranges and needn't reach their ends.
All inputs are finite; a program needn't handle non-finite values.
Results may differ from the reference program's by a relative error of at most 0.023.
Values may be sent and summed in bfloat16 or wider, within the bound.
No kernel may reach another device: no remote copies, remote signals or barrier semaphores. Data moves between devices by JAX's collectives and lax.ppermute only.
A program may use at most 64 MiB of HBM per device.

```python
import math
import jax
import jax.numpy as jnp
from jax import lax

D = 4096
C = 4096
TAPS = 3
MICROS = 16
SLICE = 512
SECTIONS = 16
N_TENSOR = 32


def draw_x_in(key, part):
    key_base, key_rows, key_cols = jax.random.split(jax.random.fold_in(key, 11), 3)
    shape = (SECTIONS, SLICE, D)
    row_scale = jnp.exp(jax.random.uniform(key_rows, (SECTIONS, SLICE, 1), jnp.float32, math.log(0.3), math.log(3.0)))
    col_scale = jnp.exp(jax.random.uniform(key_cols, (SECTIONS, 1, D), jnp.float32, math.log(0.3), math.log(3.0)))
    base = jnp.clip(jax.random.normal(key_base, shape, jnp.float32), -4.0, 4.0)
    return (base * row_scale * col_scale).astype(jnp.bfloat16)


def draw_grad_out(key, part):
    key_base, key_rows = jax.random.split(jax.random.fold_in(key, 23), 2)
    shape = (SECTIONS, SLICE, D)
    position = jnp.arange(SLICE, dtype=jnp.float32) / max(SLICE - 1, 1)
    jitter = jnp.exp(jax.random.uniform(key_rows, (SECTIONS, SLICE, 1), jnp.float32, math.log(0.7), math.log(1.4)))
    rising = 1.0 + 2.0 * position
    base = jnp.clip(jax.random.normal(key_base, shape, jnp.float32), -4.0, 4.0)
    return (base * rising[None, :, None] * jitter).astype(jnp.bfloat16)


def with_ends(entries, stream_key, low, largest):
    longest = entries.shape.index(max(entries.shape))
    spots = []
    for shift in (0, 1):
        where = [jax.random.randint(jax.random.fold_in(stream_key, axis), (), 0, length) for axis, length in enumerate(entries.shape)]
        where[longest] = (where[longest] + shift) % entries.shape[longest]
        spots.append(tuple(where))
    return entries.at[spots[0]].set(low).at[spots[1]].set(largest)


def block_levels(rng, extent, cuts, least, largest):
    level = 1.0
    for axis_at, shards_of in cuts:
        steps = jax.random.uniform(jax.random.fold_in(jax.random.fold_in(rng, 6), axis_at), (shards_of,), jnp.float32, least / len(cuts), largest / len(cuts))
        level = level * jnp.repeat(jnp.exp(steps), extent[axis_at] // shards_of).reshape((-1,) + (1,) * (len(extent) - 1 - axis_at))
    return level


def scatter_about(own_key, dims, width, limit, pieces=(), kind=jnp.bfloat16):
    entries = jax.random.normal(own_key, dims, jnp.float32) * width
    if len(pieces) > 0:
        entries = block_levels(own_key, dims, pieces, -0.22, 0.18) * entries
    return jnp.clip(entries, min=-limit, max=limit).astype(kind)


def setup_inputs(seed: int = 0) -> dict:
    key_list = jax.random.split(jax.random.key(seed), 9)
    x_in = draw_x_in(jax.random.fold_in(key_list[8], 71), 0)
    grad_out = draw_grad_out(jax.random.fold_in(key_list[8], 71), 0)
    gain = jnp.clip(1.0 + 0.1 * jax.random.normal(key_list[2], (SECTIONS, D), jnp.float32), 0.5, 1.5)
    w_val = scatter_about(key_list[3], (SECTIONS, C, D), D ** -0.5, 0.09375, ((0, 16), (1, 32)))
    w_out = scatter_about(key_list[4], (SECTIONS, C, D), C ** -0.5, 0.09375, ((0, 16), (1, 32)))
    filt = scatter_about(key_list[5], (SECTIONS, TAPS, C), 0.5, 3.0, ((0, 16), (2, 32)), jnp.float32)
    tail = scatter_about(key_list[6], (SECTIONS, TAPS - 1, C), 1.0, 6.0, ((0, 16), (2, 32)))
    micro_index = with_ends(jax.random.randint(key_list[7], (SECTIONS,), 0, MICROS), jax.random.fold_in(key_list[7], 1), 0, MICROS - 1).astype(jnp.int32)
    return dict(x_in=x_in, grad_out=grad_out, gain=gain, w_val=w_val, w_out=w_out, filt=filt, tail=tail, micro_index=micro_index)


EPSILON = 1e-06

def section_backward(x_in, grad_out, gain, w_val, w_out, filt, tail, micro_now):
    seq_len = x_in.shape[0]
    local_ch = C // N_TENSOR
    x_float = x_in.astype(jnp.float32)
    inv_rms = lax.rsqrt(lax.optimization_barrier(jnp.mean(x_float * x_float, axis=-1, keepdims=True)) + EPSILON)
    normed = (x_float * inv_rms * gain).astype(jnp.bfloat16)
    values = jnp.dot(normed, w_val.T, preferred_element_type=jnp.float32).astype(jnp.bfloat16)
    has_tail = micro_now > 0
    lead_rows = jnp.where(has_tail, tail, jnp.zeros_like(tail))
    extended = jnp.concatenate([lead_rows, values], axis=0).astype(jnp.float32)
    conv_out = filt[0] * extended[TAPS - 1:TAPS - 1 + seq_len]
    for tap in range(1, TAPS):
        conv_out = conv_out + filt[tap] * extended[TAPS - 1 - tap:TAPS - 1 - tap + seq_len]
    gate_sig = jax.nn.sigmoid(conv_out)
    gated = (conv_out * gate_sig).astype(jnp.bfloat16)
    grad_gated = jnp.dot(grad_out, w_out.T, preferred_element_type=jnp.float32)
    grad_conv = grad_gated * gate_sig * (1.0 + conv_out * (1.0 - gate_sig))
    grad_filter = jnp.stack([lax.optimization_barrier(jnp.sum(grad_conv * extended[TAPS - 1 - tap:TAPS - 1 - tap + seq_len], axis=0)) for tap in range(TAPS)])
    padded = jnp.pad(grad_conv, ((TAPS - 1, TAPS - 1), (0, 0)))
    grad_ext = filt[0] * padded[0:seq_len + TAPS - 1]
    for tap in range(1, TAPS):
        grad_ext = grad_ext + filt[tap] * padded[tap:tap + seq_len + TAPS - 1]
    grad_values = grad_ext[TAPS - 1:].astype(jnp.bfloat16)
    grad_tail = jnp.where(has_tail, grad_ext[:TAPS - 1], jnp.zeros_like(grad_ext[:TAPS - 1]))
    grad_w_out = jnp.dot(gated.T, grad_out, preferred_element_type=jnp.float32).astype(jnp.bfloat16)
    grad_w_val = jnp.dot(grad_values.T, normed, preferred_element_type=jnp.float32).astype(jnp.bfloat16)

    def add_block(total, index):
        start = (index * local_ch).astype(jnp.int32)
        grad_part = lax.dynamic_slice_in_dim(grad_values, start, local_ch, 1)
        weight_part = lax.dynamic_slice_in_dim(w_val, start, local_ch, 0)
        product = jnp.dot(grad_part, weight_part, preferred_element_type=jnp.float32)
        product = lax.optimization_barrier(product.astype(jnp.bfloat16)).astype(jnp.float32)
        return (total + product, None)
    grad_normed, _ = lax.scan(add_block, jnp.zeros((seq_len, D), jnp.float32), jnp.arange(N_TENSOR, dtype=jnp.int32))
    grad_gain = lax.optimization_barrier(jnp.sum(grad_normed * x_float * inv_rms, axis=0))
    scaled = gain * grad_normed
    grad_local = grad_out.astype(jnp.float32) + inv_rms * scaled - x_float * inv_rms ** 3 * lax.optimization_barrier(jnp.mean(scaled * x_float, axis=-1, keepdims=True))
    return (grad_local.astype(jnp.bfloat16), grad_w_val, grad_w_out, grad_filter, grad_tail, grad_gain)

def apply_section(section_args):
    return section_backward(*section_args)

def reference(x_in, grad_out, gain, w_val, w_out, filt, tail, micro_index):
    results = lax.map(apply_section, (x_in, grad_out, gain, w_val, w_out, filt, tail, micro_index))
    grad_local, grad_w_val, grad_w_out, grad_filter, grad_tail, grad_gain = results
    return (jnp.roll(grad_local, -1, axis=0), grad_w_val, grad_w_out, grad_filter, grad_tail, grad_gain)
```

```python
import jax
import jax.numpy as jnp
from jax import lax
from jax.sharding import Mesh, PartitionSpec as P

TAPS = 3
EPSILON = 1e-06
Y, Z, CORE = 8, 2, 2
TENSOR = ("y", "z", "core")
F32, BF16 = jnp.float32, jnp.bfloat16


def contract(left, right, dims):
    return lax.dot_general(left, right, (dims, ((), ())), preferred_element_type=F32)


def to_previous(block, flip_z=False):
    sections = lax.axis_size("section")
    route = []
    for s in range(sections):
        for z in range(Z):
            target = ((s - 1) % sections, 1 - z if flip_z else z)
            route.append((s * Z + z, target[0] * Z + target[1]))
    return lax.ppermute(block, ("section", "z"), route)


def summed_in_pairs(total, steps):
    for axis, apart in steps:
        devices = range(lax.axis_size(axis))
        total = total + lax.ppermute(total, axis, [(i, i ^ apart) for i in devices])
    return total


def on_device(x_in, grad_out, gain, w_val, w_out, filt, tail, micro_index):
    x_rows, cot_rows, gain_row = x_in[0], grad_out[0], gain[0]
    val_weight, out_weight = w_val[0], w_out[0]
    filters, tail_rows = filt[0], tail[0]
    has_tail = micro_index[0] > 0
    rows, width = x_rows.shape
    channels = val_weight.shape[0]
    tokens = rows * Y * Z * CORE

    x_float = x_rows.astype(F32)
    inv_rms = lax.rsqrt(jnp.mean(x_float * x_float, axis=-1, keepdims=True) + EPSILON)
    normed = (x_float * inv_rms * gain_row).astype(BF16)
    both = jnp.concatenate([normed, cot_rows], axis=0)
    both = lax.all_gather(both, "z", axis=0, tiled=True)
    both = lax.all_gather(both, ("y", "core"), axis=0, tiled=True)

    next_rows = to_previous(jnp.concatenate([x_rows, cot_rows], axis=0))
    next_gain = to_previous(gain_row[None])

    weights = jnp.concatenate([val_weight, out_weight], axis=0)
    products = contract(both, weights, ((1,), (1,)))
    products = products.reshape(Y, CORE, Z, 2, rows, 2, channels)

    def in_token_order(block):
        return block.transpose(0, 2, 1, 3, 4).reshape(tokens, channels)

    values = in_token_order(products[:, :, :, 0, :, 0]).astype(BF16)
    grad_gated = in_token_order(products[:, :, :, 1, :, 1])

    lead_rows = jnp.where(has_tail, tail_rows, jnp.zeros_like(tail_rows))
    extended = jnp.concatenate([lead_rows, values], axis=0).astype(F32)
    conv_out = filters[0] * extended[TAPS - 1 : TAPS - 1 + tokens]
    for tap in range(1, TAPS):
        conv_out = conv_out + filters[tap] * extended[TAPS - 1 - tap : TAPS - 1 - tap + tokens]
    gate_sig = jax.nn.sigmoid(conv_out)
    gated = (conv_out * gate_sig).astype(BF16)
    grad_conv = grad_gated * gate_sig * (1.0 + conv_out * (1.0 - gate_sig))
    grad_filter = jnp.stack(
        [
            jnp.sum(grad_conv * extended[TAPS - 1 - tap : TAPS - 1 - tap + tokens], axis=0)
            for tap in range(TAPS)
        ]
    )
    padded = jnp.pad(grad_conv, ((TAPS - 1, TAPS - 1), (0, 0)))
    grad_ext = filters[0] * padded[0 : tokens + TAPS - 1]
    for tap in range(1, TAPS):
        grad_ext = grad_ext + filters[tap] * padded[tap : tap + tokens + TAPS - 1]
    grad_values = grad_ext[TAPS - 1 :].astype(BF16)
    grad_tail = jnp.where(has_tail, grad_ext[: TAPS - 1], jnp.zeros_like(grad_ext[: TAPS - 1]))

    placed = grad_values.reshape(Y, Z, CORE, rows, channels)
    placed = jnp.where(lax.axis_index("z") == 0, placed, placed[:, ::-1])
    placed = placed.transpose(2, 0, 1, 3, 4).reshape(CORE, tokens // CORE, channels)
    own_core = lax.axis_index("core") == 0
    kept = jnp.where(own_core, placed[0], placed[1])
    given = jnp.where(own_core, placed[1], placed[0])
    share = contract(given, val_weight, ((1,), (0,))).astype(BF16)
    share = lax.ppermute(share, "core", [(0, 1), (1, 0)])
    share = contract(kept, val_weight, ((1,), (0,))) + share.astype(F32)
    share = lax.psum_scatter(share.astype(BF16), "y", scatter_dimension=0, tiled=True)

    def in_gathered_order(block):
        return block.reshape(Y, Z, CORE, rows, channels).transpose(0, 2, 1, 3, 4)

    zeros = jnp.zeros((Y, CORE, Z, rows, channels), BF16)
    factors = jnp.stack(
        [
            jnp.concatenate([in_gathered_order(grad_values), zeros], axis=-1),
            jnp.concatenate([zeros, in_gathered_order(gated)], axis=-1),
        ],
        axis=3,
    ).reshape(2 * tokens, 2 * channels)
    grad_weights = contract(factors, both, ((0,), (0,)))
    grad_wv, grad_wo = grad_weights[:channels], grad_weights[channels:]
    gain_term = jnp.sum(grad_wv * val_weight.astype(F32), axis=0) / gain_row
    grad_gain = summed_in_pairs(gain_term[None], (("core", 1), ("z", 1), ("y", 1), ("y", 2), ("y", 4)))

    grad_normed = to_previous(share[:rows]).astype(F32) + to_previous(share[rows:], True).astype(F32)
    x_float = next_rows[:rows].astype(F32)
    cot_float = next_rows[rows:].astype(F32)
    inv_rms = lax.rsqrt(jnp.mean(x_float * x_float, axis=-1, keepdims=True) + EPSILON)
    scaled = next_gain * grad_normed
    received = (
        cot_float
        + inv_rms * scaled
        - x_float * inv_rms**3 * jnp.mean(scaled * x_float, axis=-1, keepdims=True)
    ).astype(BF16)
    return (
        received[None],
        grad_wv.astype(BF16)[None],
        grad_wo.astype(BF16)[None],
        grad_filter[None],
        grad_tail[None],
        grad_gain,
    )


def solution(mesh):
    sections = mesh.shape["section"]
    split = Mesh(mesh.devices.reshape(sections, Y, Z, CORE), ("section", *TENSOR))
    by_rows = P("section", TENSOR, None)
    by_columns = P("section", None, TENSOR)
    whole = P("section", None)
    return jax.shard_map(
        on_device,
        mesh=split,
        in_specs=(by_rows, by_rows, whole, by_rows, by_rows, by_columns, by_columns, P("section")),
        out_specs=(by_rows, by_rows, by_rows, by_columns, by_columns, whole),
        check_vma=False,
    )
```

```python
import jax
import jax.numpy as jnp
from jax import lax
from jax.sharding import Mesh, PartitionSpec as P

TAPS = 3
EPSILON = 1e-06
Y, Z, CORE = 8, 2, 2
TENSOR = ("y", "z", "core")
SWAP = ((0, 1), (1, 0))
F32, BF16 = jnp.float32, jnp.bfloat16


def contract(left, right, dims):
    return lax.dot_general(left, right, (dims, ((), ())), preferred_element_type=F32)


def to_previous(block, flip_z=False):
    sections = lax.axis_size("section")
    route = []
    for s in range(sections):
        for z in range(Z):
            target = ((s - 1) % sections, 1 - z if flip_z else z)
            route.append((s * Z + z, target[0] * Z + target[1]))
    return lax.ppermute(block, ("section", "z"), route)


def summed_in_pairs(total, steps):
    for axis, apart in steps:
        devices = range(lax.axis_size(axis))
        total = total + lax.ppermute(total, axis, [(i, i ^ apart) for i in devices])
    return total


def on_device(x_in, grad_out, gain, w_val, w_out, filt, tail, micro_index):
    x_rows, cot_rows, gain_row = x_in[0], grad_out[0], gain[0]
    val_weight, out_weight = w_val[0], w_out[0]
    filters, tail_rows = filt[0], tail[0]
    has_tail = micro_index[0] > 0
    rows, width = x_rows.shape
    channels = val_weight.shape[0]
    tokens = rows * Y * Z * CORE

    x_float = x_rows.astype(F32)
    inv_rms = lax.rsqrt(jnp.mean(x_float * x_float, axis=-1, keepdims=True) + EPSILON)
    normed = (x_float * inv_rms * gain_row).astype(BF16)
    both = jnp.concatenate([normed, cot_rows], axis=0)
    both = lax.all_gather(both, "z", axis=0, tiled=True)
    both = lax.all_gather(both, ("y", "core"), axis=0, tiled=True)

    next_rows = to_previous(jnp.concatenate([x_rows, cot_rows], axis=0))
    next_gain = to_previous(gain_row[None])
    pair_weight = lax.ppermute(val_weight, "core", SWAP)
    both, next_rows, next_gain, pair_weight = lax.optimization_barrier((both, next_rows, next_gain, pair_weight))

    weights = jnp.concatenate([val_weight, out_weight], axis=0)
    products = contract(both, weights, ((1,), (1,)))
    products = products.reshape(Y, CORE, Z, 2, rows, 2, channels)

    def in_token_order(block):
        return block.transpose(0, 2, 1, 3, 4).reshape(tokens, channels)

    values = in_token_order(products[:, :, :, 0, :, 0]).astype(BF16)
    grad_gated = in_token_order(products[:, :, :, 1, :, 1])

    lead_rows = jnp.where(has_tail, tail_rows, jnp.zeros_like(tail_rows))
    extended = jnp.concatenate([lead_rows, values], axis=0).astype(F32)
    conv_out = filters[0] * extended[TAPS - 1 : TAPS - 1 + tokens]
    for tap in range(1, TAPS):
        conv_out = conv_out + filters[tap] * extended[TAPS - 1 - tap : TAPS - 1 - tap + tokens]
    gate_sig = jax.nn.sigmoid(conv_out)
    gated = (conv_out * gate_sig).astype(BF16)
    grad_conv = grad_gated * gate_sig * (1.0 + conv_out * (1.0 - gate_sig))
    grad_filter = jnp.stack(
        [
            jnp.sum(grad_conv * extended[TAPS - 1 - tap : TAPS - 1 - tap + tokens], axis=0)
            for tap in range(TAPS)
        ]
    )
    padded = jnp.pad(grad_conv, ((TAPS - 1, TAPS - 1), (0, 0)))
    grad_ext = filters[0] * padded[0 : tokens + TAPS - 1]
    for tap in range(1, TAPS):
        grad_ext = grad_ext + filters[tap] * padded[tap : tap + tokens + TAPS - 1]
    grad_values = grad_ext[TAPS - 1 :].astype(BF16)
    grad_tail = jnp.where(has_tail, grad_ext[: TAPS - 1], jnp.zeros_like(grad_ext[: TAPS - 1]))

    placed = grad_values.reshape(Y, Z, CORE, rows, channels)
    placed = jnp.where(lax.axis_index("z") == 0, placed, placed[:, ::-1])
    placed = placed.transpose(2, 0, 1, 3, 4).reshape(CORE, tokens // CORE, channels)
    own_core = lax.axis_index("core") == 0
    kept = jnp.where(own_core, placed[0], placed[1])
    given = jnp.where(own_core, placed[1], placed[0])
    taken = lax.ppermute(given, "core", SWAP)
    share = contract(
        jnp.concatenate([kept, taken], axis=1),
        jnp.concatenate([val_weight, pair_weight], axis=0),
        ((1,), (0,)),
    )
    share = lax.psum_scatter(share.astype(BF16), "y", scatter_dimension=0, tiled=True)

    def in_gathered_order(block):
        return block.reshape(Y, Z, CORE, rows, channels).transpose(0, 2, 1, 3, 4)

    zeros = jnp.zeros((Y, CORE, Z, rows, channels), BF16)
    factors = jnp.stack(
        [
            jnp.concatenate([in_gathered_order(grad_values), zeros], axis=-1),
            jnp.concatenate([zeros, in_gathered_order(gated)], axis=-1),
        ],
        axis=3,
    ).reshape(2 * tokens, 2 * channels)
    grad_weights = contract(factors, both, ((0,), (0,)))
    grad_wv, grad_wo = grad_weights[:channels], grad_weights[channels:]
    gain_term = jnp.sum(grad_wv * val_weight.astype(F32), axis=0) / gain_row
    grad_gain = summed_in_pairs(gain_term[None], (("core", 1), ("z", 1), ("y", 1), ("y", 2), ("y", 4)))

    share, grad_gain = lax.optimization_barrier((share, grad_gain))

    grad_normed = to_previous(share[:rows]).astype(F32) + to_previous(share[rows:], True).astype(F32)
    x_float = next_rows[:rows].astype(F32)
    cot_float = next_rows[rows:].astype(F32)
    inv_rms = lax.rsqrt(jnp.mean(x_float * x_float, axis=-1, keepdims=True) + EPSILON)
    scaled = next_gain * grad_normed
    received = (
        cot_float
        + inv_rms * scaled
        - x_float * inv_rms**3 * jnp.mean(scaled * x_float, axis=-1, keepdims=True)
    ).astype(BF16)
    return (
        received[None],
        grad_wv.astype(BF16)[None],
        grad_wo.astype(BF16)[None],
        grad_filter[None],
        grad_tail[None],
        grad_gain,
    )


def solution(mesh):
    sections = mesh.shape["section"]
    split = Mesh(mesh.devices.reshape(sections, Y, Z, CORE), ("section", *TENSOR))
    by_rows = P("section", TENSOR, None)
    by_columns = P("section", None, TENSOR)
    whole = P("section", None)
    return jax.shard_map(
        on_device,
        mesh=split,
        in_specs=(by_rows, by_rows, whole, by_rows, by_rows, by_columns, by_columns, P("section")),
        out_specs=(by_rows, by_rows, by_rows, by_columns, by_columns, whole),
        check_vma=False,
    )
```

```python
import jax
import jax.numpy as jnp
from jax import lax
from jax.sharding import Mesh, PartitionSpec as P

TAPS = 3
EPSILON = 1e-06
Y, Z, CORE = 8, 2, 2
TENSOR = ("y", "z", "core")
SWAP = ((0, 1), (1, 0))
F32, BF16 = jnp.float32, jnp.bfloat16


def contract(left, right, dims):
    return lax.dot_general(left, right, (dims, ((), ())), preferred_element_type=F32)


def along(block, axis, distance):
    devices = lax.axis_size(axis)
    return lax.ppermute(block, axis, [(i, (i + distance) % devices) for i in range(devices)])


def summed_in_pairs(total, steps):
    for axis, apart in steps:
        devices = range(lax.axis_size(axis))
        total = total + lax.ppermute(total, axis, [(i, i ^ apart) for i in devices])
    return total


def own_first(pair, axis):
    return jnp.where(lax.axis_index(axis) == 0, pair, pair[::-1])


def from_own_y(block):
    return lax.dynamic_slice_in_dim(jnp.concatenate([block, block]), lax.axis_index("y"), Y)


def from_first_y(block):
    return lax.dynamic_slice_in_dim(jnp.concatenate([block, block]), (Y - lax.axis_index("y")) % Y, Y)


def gathered(own, mate):
    found = {(0, 0): own, (1, 0): mate}
    ahead, behind = [own, mate], [own, mate]
    half = Y // 2
    for step in range(1, half):
        for z in range(Z):
            ahead[z] = along(ahead[z], "y", -1)
            behind[z] = along(behind[z], "y", 1)
            found[z, step], found[z, Y - step] = ahead[z], behind[z]
    found[0, half] = along(ahead[0], "y", -1)
    found[1, half] = along(behind[1], "y", 1)
    return found


def reduced(share):
    half = Y // 2
    up, down = share[half], share[half + 1]
    for step in range(1, half):
        up = along(up, "y", 1)
        up = (share[half - step].astype(F32) + up.astype(F32)).astype(BF16)
    for step in range(half + 2, Y):
        down = along(down, "y", -1)
        down = (share[step].astype(F32) + down.astype(F32)).astype(BF16)
    return share[0].astype(F32) + along(up, "y", 1).astype(F32) + along(down, "y", -1).astype(F32)


def on_device(x_in, grad_out, gain, w_val, w_out, filt, tail, micro_index):
    x_rows, cot_rows, gain_row = x_in[0], grad_out[0], gain[0]
    val_weight, out_weight = w_val[0], w_out[0]
    filters, tail_rows = filt[0], tail[0]
    has_tail = micro_index[0] > 0
    rows, width = x_rows.shape
    channels = val_weight.shape[0]
    tokens = rows * Y * Z * CORE

    x_float = x_rows.astype(F32)
    inv_rms = lax.rsqrt(jnp.mean(x_float * x_float, axis=-1, keepdims=True) + EPSILON)
    normed = (x_float * inv_rms * gain_row).astype(BF16)

    own = jnp.concatenate([normed, cot_rows], axis=0)
    mate = lax.ppermute(own, "z", SWAP)
    blocks = gathered(own, mate)

    val_core = lax.ppermute(val_weight, "core", SWAP)
    out_core = lax.ppermute(out_weight, "core", SWAP)
    mate_done, val_sent = lax.optimization_barrier((mate, val_weight))
    val_z = lax.ppermute(val_sent, "z", SWAP)
    val_z_core = lax.ppermute(val_z, "core", SWAP)
    weights = jnp.concatenate([val_weight, val_core, out_weight, out_core], axis=0)

    def products(places):
        found = contract(jnp.concatenate([blocks[p] for p in places], axis=0), weights, ((1,), (1,)))
        found = found.reshape(len(places), 2, rows, 2, CORE, channels)
        return {p: (found[i, 0, :, 0], found[i, 1, :, 1]) for i, p in enumerate(places)}

    half = Y // 2
    early = [(z, y) for z in range(Z) for y in range(Y) if min(y, Y - y) < half - 1]
    late = [(z, y) for z in range(Z) for y in range(Y) if min(y, Y - y) >= half - 1]
    by_place = {**products(early), **products(late)}
    found = jnp.stack(
        [jnp.stack([jnp.stack([by_place[z, y][k] for y in range(Y)]) for z in range(Z)]) for k in range(2)]
    )
    kept, given = found[..., 0, :], found[..., 1, :]
    taken = lax.ppermute(given, "core", SWAP)
    found = own_first(jnp.stack([kept, taken]), "core")
    found = own_first(found.transpose(2, 0, 1, 3, 4, 5), "z")
    found = from_first_y(found.transpose(3, 0, 1, 2, 4, 5))
    found = found.transpose(3, 0, 1, 2, 4, 5).reshape(2, tokens, channels)
    values, grad_gated = found[0].astype(BF16), found[1]

    lead_rows = jnp.where(has_tail, tail_rows, jnp.zeros_like(tail_rows))
    extended = jnp.concatenate([lead_rows, values], axis=0).astype(F32)
    conv_out = filters[0] * extended[TAPS - 1 : TAPS - 1 + tokens]
    for tap in range(1, TAPS):
        conv_out = conv_out + filters[tap] * extended[TAPS - 1 - tap : TAPS - 1 - tap + tokens]
    gate_sig = jax.nn.sigmoid(conv_out)
    gated = (conv_out * gate_sig).astype(BF16)
    grad_conv = grad_gated * gate_sig * (1.0 + conv_out * (1.0 - gate_sig))
    grad_filter = jnp.stack(
        [
            jnp.sum(grad_conv * extended[TAPS - 1 - tap : TAPS - 1 - tap + tokens], axis=0)
            for tap in range(TAPS)
        ]
    )
    padded = jnp.pad(grad_conv, ((TAPS - 1, TAPS - 1), (0, 0)))
    grad_ext = filters[0] * padded[0 : tokens + TAPS - 1]
    for tap in range(1, TAPS):
        grad_ext = grad_ext + filters[tap] * padded[tap : tap + tokens + TAPS - 1]
    grad_values = grad_ext[TAPS - 1 :].astype(BF16)
    grad_tail = jnp.where(has_tail, grad_ext[: TAPS - 1], jnp.zeros_like(grad_ext[: TAPS - 1]))

    factors = jnp.concatenate([grad_values, gated], axis=-1).reshape(Y, Z, CORE, rows, 2 * channels)
    factors = from_own_y(factors).transpose(2, 1, 0, 3, 4)
    factors = own_first(factors, "core").transpose(1, 0, 2, 3, 4)
    factors = own_first(factors, "z").transpose(1, 0, 2, 3, 4)
    taken = lax.ppermute(factors[1], "core", SWAP)
    kept = factors[0]
    of_values = jnp.concatenate([kept[..., :channels], taken[..., :channels]], axis=-1)
    of_gated = jnp.concatenate([kept[..., channels:], taken[..., channels:]], axis=-1)

    taken = lax.ppermute(of_values[1], "z", SWAP)
    share = contract(
        jnp.concatenate([of_values[0], taken], axis=-1).reshape(Y * rows, 2 * CORE * channels),
        jnp.concatenate([val_weight, val_core, val_z, val_z_core], axis=0),
        ((1,), (0,)),
    )
    grad_normed = reduced(share.astype(BF16).reshape(Y, rows, width))

    zeros = jnp.zeros_like(of_values)
    sided = jnp.stack(
        [jnp.concatenate([of_values, zeros], axis=-1), jnp.concatenate([zeros, of_gated], axis=-1)], axis=2
    ).reshape(2 * tokens // CORE, 2 * CORE * channels)
    every = jnp.concatenate([blocks[z, y] for z in range(Z) for y in range(Y)], axis=0)
    grad_weights = contract(sided, every, ((0,), (0,))).reshape(2, CORE, channels, width)
    gain_term = jnp.sum(
        grad_weights[0] * jnp.stack([val_weight, val_core]).astype(F32), axis=(0, 1)
    ) / gain_row
    grad_gain = summed_in_pairs(gain_term[None], (("core", 1), ("z", 1), ("y", 1), ("y", 2), ("y", 4)))
    grad_weights = grad_weights[:, 0] + lax.ppermute(grad_weights[:, 1].astype(BF16), "core", SWAP).astype(F32)

    scaled = gain_row * grad_normed
    grad_local = (
        cot_rows.astype(F32)
        + inv_rms * scaled
        - x_float * inv_rms**3 * jnp.mean(scaled * x_float, axis=-1, keepdims=True)
    )
    received = along(grad_local.astype(BF16), "section", -1)
    return (
        received[None],
        grad_weights[0].astype(BF16)[None],
        grad_weights[1].astype(BF16)[None],
        grad_filter[None],
        grad_tail[None],
        grad_gain,
    )


def solution(mesh):
    sections = mesh.shape["section"]
    split = Mesh(mesh.devices.reshape(sections, Y, Z, CORE), ("section", *TENSOR))
    by_rows = P("section", TENSOR, None)
    by_columns = P("section", None, TENSOR)
    whole = P("section", None)
    return jax.shard_map(
        on_device,
        mesh=split,
        in_specs=(by_rows, by_rows, whole, by_rows, by_rows, by_columns, by_columns, P("section")),
        out_specs=(by_rows, by_rows, by_rows, by_columns, by_columns, whole),
        check_vma=False,
    )
```

```python
import jax
import jax.numpy as jnp
from jax import lax
from jax.experimental import pallas as pl
from jax.experimental.pallas import tpu as pltpu
from jax.sharding import Mesh, PartitionSpec as P

TAPS = 3
EPSILON = 1e-06
Y, Z, CORE = 8, 2, 2
TENSOR = ("y", "z", "core")
SWAP = ((0, 1), (1, 0))
F32, BF16 = jnp.float32, jnp.bfloat16


def contract(left, right, dims):
    return lax.dot_general(left, right, (dims, ((), ())), preferred_element_type=F32)


def along(block, axis, distance):
    devices = lax.axis_size(axis)
    return lax.ppermute(block, axis, [(i, (i + distance) % devices) for i in range(devices)])


def with_partner(total, axis, apart):
    devices = range(lax.axis_size(axis))
    return total + lax.ppermute(total, axis, [(i, i ^ apart) for i in devices])


def gathered(own):
    half, rows = Y // 2, own.shape[0] // 2
    found = {0: own}
    ahead = behind = own
    for step in range(1, half):
        ahead, behind = along(ahead, "y", -1), along(behind, "y", 1)
        found[step], found[Y - step] = ahead, behind
    found[half] = (along(ahead[:rows], "y", -1), along(behind[rows:], "y", 1))
    return found


def reduced(share, partial):
    half = Y // 2
    up, down = along(share[half], "y", 1), share[half + 1]
    up, partial = lax.optimization_barrier((up, partial))
    kept_val, kept_out, given, total = partial
    taken = lax.ppermute(given, "core", SWAP)
    beside = ((("core", 1), ("z", 1)), (("y", 1),), (("y", 2),))
    for step in range(1, half):
        up = along((share[half - step].astype(F32) + up.astype(F32)).astype(BF16), "y", 1)
        if step > 1:
            down = (share[half + step].astype(F32) + down.astype(F32)).astype(BF16)
        down = along(down, "y", -1)
        for axis, apart in beside[step - 1]:
            total = with_partner(total, axis, apart)
        up, down, total = lax.optimization_barrier((up, down, total))
    up, taken = lax.optimization_barrier((up, taken))
    grad_wv = (kept_val + taken[0].astype(F32)).astype(BF16)
    grad_wo = (kept_out + taken[1].astype(F32)).astype(BF16)
    return share[0].astype(F32) + up.astype(F32) + down.astype(F32), grad_wv, grad_wo, total


def vmem_params(mib):
    return pltpu.CompilerParams(vmem_limit_bytes=mib << 20)


def sorted_products(products, rows, channels):
    def body(*refs):
        kept, given = refs[-2:]
        for y in range(Y):
            for z in range(Z):
                for kind in range(2):
                    if y < Y // 2:
                        source, at = refs[y], (2 * z + kind) * rows
                    elif y > Y // 2:
                        source, at = refs[y + 1], (2 * z + kind) * rows
                    else:
                        source, at = refs[y + z], kind * rows
                    for core, target in enumerate((kept, given)):
                        column = (2 * kind + core) * channels
                        target[kind, z, y] = source[at : at + rows, column : column + channels]

    operands = [*products[: Y // 2], *products[Y // 2], *products[Y // 2 + 1 :]]
    shape = jax.ShapeDtypeStruct((2, Z, Y, rows, channels), F32)
    return pl.pallas_call(
        body,
        out_shape=(shape, shape),
        compiler_params=vmem_params(16),
        cost_estimate=pl.CostEstimate(flops=0, bytes_accessed=4 << 20, transcendentals=0),
        name="sorted_products",
    )(*operands)


def through_gate(place, kept, taken, filters, lead_rows):
    rows, channels = kept.shape[-2:]
    tokens = rows * Y * Z * CORE
    edge = 8

    def body(place, kept, taken, filters, lead, own, other, near_z, grad_filter, grad_lead, ext, cot, back, val, gat):
        def start(core, z, y):
            at_y = lax.rem(place[0] + y, Y)
            at_z = place[1] if z == 0 else 1 - place[1]
            at_core = place[2] if core == 0 else 1 - place[2]
            return pl.multiple_of(((at_y * Z + at_z) * CORE + at_core) * rows, rows)

        ext[0:edge] = jnp.zeros((edge, channels), F32)
        ext[edge - TAPS + 1 : edge] = lead[...]
        for core, source in enumerate((kept, taken)):
            for z in range(Z):
                for y in range(Y):
                    at = start(core, z, y)
                    ext[pl.ds(edge + at, rows)] = source[0, z, y].astype(BF16).astype(F32)
                    cot[pl.ds(at, rows)] = source[1, z, y]
        taps = [filters[k : k + 1, :] for k in range(TAPS)]
        delayed = [ext[edge - k : edge - k + tokens] for k in range(TAPS)]
        conv_out = taps[0] * delayed[0]
        for k in range(1, TAPS):
            conv_out = conv_out + taps[k] * delayed[k]
        gate_sig = jax.nn.sigmoid(conv_out)
        gat[...] = (conv_out * gate_sig).astype(BF16)
        grad_conv = cot[...] * gate_sig * (1.0 + conv_out * (1.0 - gate_sig))
        for k in range(TAPS):
            grad_filter[k : k + 1, :] = jnp.sum(grad_conv * delayed[k], axis=0, keepdims=True)
        back[0:edge] = jnp.zeros((edge, channels), F32)
        back[edge + tokens : edge + tokens + edge] = jnp.zeros((edge, channels), F32)
        back[edge : edge + tokens] = grad_conv
        grad_values = taps[0] * back[edge : edge + tokens]
        first = edge - TAPS + 1
        grad_head = taps[0] * back[first:edge]
        for k in range(1, TAPS):
            grad_values = grad_values + taps[k] * back[edge + k : edge + k + tokens]
            grad_head = grad_head + taps[k] * back[first + k : edge + k]
        grad_lead[...] = grad_head
        val[...] = grad_values.astype(BF16)
        for z in range(Z):
            for y in range(Y):
                block = slice(y * rows, (y + 1) * rows)
                at = start(0, z, y)
                own[0, z, block] = val[pl.ds(at, rows)]
                own[1, z, block] = gat[pl.ds(at, rows)]
                if z == 1:
                    near_z[0, block] = val[pl.ds(at, rows)]
                at = start(1, z, y)
                other[0, z, block] = val[pl.ds(at, rows)]
                other[1, z, block] = gat[pl.ds(at, rows)]
                if z == 1:
                    near_z[1, block] = val[pl.ds(at, rows)]

    vmem = pl.BlockSpec(memory_space=pltpu.VMEM)
    quarter = (Y * rows, channels)
    return pl.pallas_call(
        body,
        in_specs=[pl.BlockSpec(memory_space=pltpu.SMEM)] + [vmem] * 4,
        out_specs=[vmem] * 5,
        out_shape=(
            jax.ShapeDtypeStruct((2, Z, *quarter), BF16),
            jax.ShapeDtypeStruct((2, Z, *quarter), BF16),
            jax.ShapeDtypeStruct((CORE, *quarter), BF16),
            jax.ShapeDtypeStruct((TAPS, channels), F32),
            jax.ShapeDtypeStruct((TAPS - 1, channels), F32),
        ),
        scratch_shapes=[
            pltpu.VMEM((edge + tokens, channels), F32),
            pltpu.VMEM((tokens, channels), F32),
            pltpu.VMEM((edge + tokens + edge, channels), F32),
            pltpu.VMEM((tokens, channels), BF16),
            pltpu.VMEM((tokens, channels), BF16),
        ],
        compiler_params=vmem_params(16),
        cost_estimate=pl.CostEstimate(flops=4 << 20, bytes_accessed=4 << 20, transcendentals=1 << 16),
        name="through_gate",
    )(place, kept, taken, filters, lead_rows)


def weight_gradients(found, own, taken, val_pair, gain_row, rows):
    width = gain_row.shape[-1]
    channels = own.shape[-1]
    column = 512

    def body(*refs):
        blocks, (own, taken, val_own, val_core, gain, *kept, given, term) = refs[: Y + 1], refs[Y + 1 :]

        def rows_of(kind):
            parts = []
            for z in range(Z):
                for y in range(Y):
                    at = (2 * z + kind) * rows
                    if y < Y // 2:
                        parts.append(blocks[y][at : at + rows])
                    elif y > Y // 2:
                        parts.append(blocks[y + 1][at : at + rows])
                    else:
                        parts.append(blocks[y + z][kind * rows : (kind + 1) * rows])
            return jnp.concatenate(parts, axis=0)

        for kind in range(2):
            factor = jnp.concatenate(
                [ref[kind].reshape(Z * Y * rows, channels) for ref in (own, taken)], axis=1
            )
            grad = contract(factor, rows_of(kind), ((0,), (0,)))
            kept[kind][...] = grad[:channels]
            given[kind] = grad[channels:].astype(BF16)
            if kind == 0:
                total = jnp.sum(grad[:channels] * val_own[...].astype(F32), axis=0, keepdims=True)
                total += jnp.sum(grad[channels:] * val_core[...].astype(F32), axis=0, keepdims=True)
                term[...] = total / gain[...]

    operands = [found[y] for y in range(Y // 2)] + list(found[Y // 2]) + [found[y] for y in range(Y // 2 + 1, Y)]
    by_column = lambda count: pl.BlockSpec((count, column), lambda i: (0, i))
    whole = pl.BlockSpec(own.shape, lambda i: (0, 0, 0, 0))
    stacked = pl.BlockSpec((2, channels, column), lambda i: (0, 0, i))
    return pl.pallas_call(
        body,
        grid=(width // column,),
        in_specs=[by_column(o.shape[0]) for o in operands]
        + [whole, whole, by_column(channels), by_column(channels), by_column(1)],
        out_specs=[by_column(channels), by_column(channels), stacked, by_column(1)],
        out_shape=(
            jax.ShapeDtypeStruct((channels, width), F32),
            jax.ShapeDtypeStruct((channels, width), F32),
            jax.ShapeDtypeStruct((2, channels, width), BF16),
            jax.ShapeDtypeStruct((1, width), F32),
        ),
        compiler_params=vmem_params(24),
        cost_estimate=pl.CostEstimate(flops=1 << 30, bytes_accessed=13 << 20, transcendentals=0),
        name="weight_gradients",
    )(*operands, own, taken, *val_pair, gain_row)


def on_device(x_in, grad_out, gain, w_val, w_out, filt, tail, micro_index):
    x_rows, cot_rows, gain_row = x_in[0], grad_out[0], gain[0]
    val_weight, out_weight = w_val[0], w_out[0]
    filters, tail_rows = filt[0], tail[0]
    has_tail = micro_index[0] > 0
    rows, width = x_rows.shape
    channels = val_weight.shape[0]

    x_float = x_rows.astype(F32)
    inv_rms = lax.rsqrt(jnp.mean(x_float * x_float, axis=-1, keepdims=True) + EPSILON)
    normed = (x_float * inv_rms * gain_row).astype(BF16)

    own = jnp.concatenate([normed, cot_rows], axis=0)
    mate = lax.ppermute(own, "z", SWAP)
    found = gathered(jnp.concatenate([own, mate], axis=0))

    val_core = lax.ppermute(val_weight, "core", SWAP)
    out_core = lax.ppermute(out_weight, "core", SWAP)
    val_sent, mate_done = lax.optimization_barrier((val_weight, mate))
    val_z = lax.ppermute(val_sent, "z", SWAP)
    val_z_core = lax.ppermute(val_z, "core", SWAP)
    weights = lax.optimization_barrier(
        jnp.concatenate([val_weight, val_core, out_weight, out_core], axis=0)
    )

    def product(block):
        return contract(block, weights, ((1,), (1,)))

    products = [
        tuple(product(b) for b in found[y]) if y == Y // 2 else product(found[y]) for y in range(Y)
    ]
    kept, given = sorted_products(products, rows, channels)
    taken = lax.ppermute(given, "core", SWAP)
    val_z, val_z_core, kept = lax.optimization_barrier((val_z, val_z_core, kept))
    val_weights = jnp.concatenate([val_weight, val_core, val_z, val_z_core], axis=0)
    val_weights, kept = lax.optimization_barrier((val_weights, kept))

    place = jnp.stack([lax.axis_index(axis) for axis in TENSOR]).astype(jnp.int32)
    lead_rows = jnp.where(has_tail, tail_rows, jnp.zeros_like(tail_rows)).astype(F32)
    own, other, near_z, grad_filter, grad_lead = through_gate(place, kept, taken, filters, lead_rows)
    grad_tail = jnp.where(has_tail, grad_lead, jnp.zeros_like(grad_lead))

    near_z_core = near_z[1]
    taken = lax.ppermute(other, "core", SWAP)
    from_z = lax.ppermute(near_z[0], "z", SWAP)
    from_z_core = lax.ppermute(near_z_core, ("z", "core"), [(i, i ^ 3) for i in range(Z * CORE)])
    share = contract(
        jnp.concatenate([own[0, 0], taken[0, 0], from_z, from_z_core], axis=1), val_weights, ((1,), (0,))
    )
    partial = weight_gradients(found, own, taken, (val_weight, val_core), gain_row[None], rows)
    grad_normed, grad_wv, grad_wo, gain_term = reduced(share.astype(BF16).reshape(Y, rows, width), partial)
    grad_gain = with_partner(gain_term, "y", 4)

    scaled = gain_row * grad_normed
    grad_local = (
        cot_rows.astype(F32)
        + inv_rms * scaled
        - x_float * inv_rms**3 * jnp.mean(scaled * x_float, axis=-1, keepdims=True)
    )
    received = along(grad_local.astype(BF16), "section", -1)
    return (
        received[None],
        grad_wv[None],
        grad_wo[None],
        grad_filter[None],
        grad_tail[None],
        grad_gain,
    )


def solution(mesh):
    sections = mesh.shape["section"]
    split = Mesh(mesh.devices.reshape(sections, Y, Z, CORE), ("section", *TENSOR))
    by_rows = P("section", TENSOR, None)
    by_columns = P("section", None, TENSOR)
    whole = P("section", None)
    return jax.shard_map(
        on_device,
        mesh=split,
        in_specs=(by_rows, by_rows, whole, by_rows, by_rows, by_columns, by_columns, P("section")),
        out_specs=(by_rows, by_rows, by_rows, by_columns, by_columns, whole),
        check_vma=False,
    )
```

```python
import jax
import jax.numpy as jnp
from jax import lax
from jax.experimental import pallas as pl
from jax.experimental.pallas import tpu as pltpu
from jax.sharding import Mesh, PartitionSpec as P


TAPS = 3
EPSILON = 1e-06
Y, Z, CORE = 8, 2, 2
TENSOR = ("y", "z", "core")
SWAP = ((0, 1), (1, 0))
F32, BF16 = jnp.float32, jnp.bfloat16


def contract(left, right, dims):
    return lax.dot_general(left, right, (dims, ((), ())), preferred_element_type=F32)


def along(block, axis, distance):
    devices = lax.axis_size(axis)
    return lax.ppermute(block, axis, [(i, (i + distance) % devices) for i in range(devices)])


def with_partner(total, axis, apart):
    devices = range(lax.axis_size(axis))
    return total + lax.ppermute(total, axis, [(i, i ^ apart) for i in devices])


def gathered(own):
    half, rows = Y // 2, own.shape[0] // 2
    found = {0: own}
    ahead = behind = own
    for step in range(1, half):
        ahead, behind = along(ahead, "y", -1), along(behind, "y", 1)
        found[step], found[Y - step] = ahead, behind
    found[half] = (along(ahead[:rows], "y", -1), along(behind[rows:], "y", 1))
    return found


def reduced(share, total):
    found = {}

    def send(apart):
        found[apart] = along(share[apart], "y", apart)

    for apart in range(1, Y):
        send(apart)
    for axis, apart in (("core", 1), ("z", 1), ("y", 1), ("y", 2)):
        total = with_partner(total, axis, apart)
    grad_normed = share[0].astype(F32)
    for apart in range(1, Y):
        grad_normed = grad_normed + found[apart].astype(F32)
    return grad_normed, total


def vmem_params(mib):
    return pltpu.CompilerParams(vmem_limit_bytes=mib << 20)


def sorted_products(products, rows, channels):
    def body(*refs):
        kept, given = refs[-2:]
        for y in range(Y):
            for z in range(Z):
                for kind in range(2):
                    if y < Y // 2:
                        source, at = refs[y], (2 * z + kind) * rows
                    elif y > Y // 2:
                        source, at = refs[y + 1], (2 * z + kind) * rows
                    else:
                        source, at = refs[y + z], kind * rows
                    for core, target in enumerate((kept, given)):
                        column = (2 * kind + core) * channels
                        target[kind, z, y] = source[at : at + rows, column : column + channels]

    operands = [*products[: Y // 2], *products[Y // 2], *products[Y // 2 + 1 :]]
    shape = jax.ShapeDtypeStruct((2, Z, Y, rows, channels), F32)
    return pl.pallas_call(
        body,
        out_shape=(shape, shape),
        compiler_params=vmem_params(16),
        cost_estimate=pl.CostEstimate(flops=0, bytes_accessed=4 << 20, transcendentals=0),
        name="sorted_products",
    )(*operands)


def through_gate(place, kept, taken, filters, lead_rows):
    rows, channels = kept.shape[-2:]
    tokens = rows * Y * Z * CORE
    edge = 8

    def body(place, kept, taken, filters, lead, own, other, near_z, grad_filter, grad_lead, ext, cot, back, val, gat):
        def start(core, z, y):
            at_y = lax.rem(place[0] + y, Y)
            at_z = place[1] if z == 0 else 1 - place[1]
            at_core = place[2] if core == 0 else 1 - place[2]
            return pl.multiple_of(((at_y * Z + at_z) * CORE + at_core) * rows, rows)

        ext[0:edge] = jnp.zeros((edge, channels), F32)
        ext[edge - TAPS + 1 : edge] = lead[...]
        for core, source in enumerate((kept, taken)):
            for z in range(Z):
                for y in range(Y):
                    at = start(core, z, y)
                    ext[pl.ds(edge + at, rows)] = source[0, z, y].astype(BF16).astype(F32)
                    cot[pl.ds(at, rows)] = source[1, z, y]
        taps = [filters[k : k + 1, :] for k in range(TAPS)]
        delayed = [ext[edge - k : edge - k + tokens] for k in range(TAPS)]
        conv_out = taps[0] * delayed[0]
        for k in range(1, TAPS):
            conv_out = conv_out + taps[k] * delayed[k]
        gate_sig = jax.nn.sigmoid(conv_out)
        gat[...] = (conv_out * gate_sig).astype(BF16)
        grad_conv = cot[...] * gate_sig * (1.0 + conv_out * (1.0 - gate_sig))
        for k in range(TAPS):
            grad_filter[k : k + 1, :] = jnp.sum(grad_conv * delayed[k], axis=0, keepdims=True)
        back[0:edge] = jnp.zeros((edge, channels), F32)
        back[edge + tokens : edge + tokens + edge] = jnp.zeros((edge, channels), F32)
        back[edge : edge + tokens] = grad_conv
        grad_values = taps[0] * back[edge : edge + tokens]
        first = edge - TAPS + 1
        grad_head = taps[0] * back[first:edge]
        for k in range(1, TAPS):
            grad_values = grad_values + taps[k] * back[edge + k : edge + k + tokens]
            grad_head = grad_head + taps[k] * back[first + k : edge + k]
        grad_lead[...] = grad_head
        val[...] = grad_values.astype(BF16)
        for z in range(Z):
            for y in range(Y):
                block = slice(y * rows, (y + 1) * rows)
                at = start(0, z, y)
                own[0, z, block] = val[pl.ds(at, rows)]
                own[1, z, block] = gat[pl.ds(at, rows)]
                if z == 1:
                    near_z[0, block] = val[pl.ds(at, rows)]
                at = start(1, z, y)
                other[0, z, block] = val[pl.ds(at, rows)]
                other[1, z, block] = gat[pl.ds(at, rows)]
                if z == 1:
                    near_z[1, block] = val[pl.ds(at, rows)]

    vmem = pl.BlockSpec(memory_space=pltpu.VMEM)
    quarter = (Y * rows, channels)
    return pl.pallas_call(
        body,
        in_specs=[pl.BlockSpec(memory_space=pltpu.SMEM)] + [vmem] * 4,
        out_specs=[vmem] * 5,
        out_shape=(
            jax.ShapeDtypeStruct((2, Z, *quarter), BF16),
            jax.ShapeDtypeStruct((2, Z, *quarter), BF16),
            jax.ShapeDtypeStruct((CORE, *quarter), BF16),
            jax.ShapeDtypeStruct((TAPS, channels), F32),
            jax.ShapeDtypeStruct((TAPS - 1, channels), F32),
        ),
        scratch_shapes=[
            pltpu.VMEM((edge + tokens, channels), F32),
            pltpu.VMEM((tokens, channels), F32),
            pltpu.VMEM((edge + tokens + edge, channels), F32),
            pltpu.VMEM((tokens, channels), BF16),
            pltpu.VMEM((tokens, channels), BF16),
        ],
        compiler_params=vmem_params(16),
        cost_estimate=pl.CostEstimate(flops=4 << 20, bytes_accessed=4 << 20, transcendentals=1 << 16),
        name="through_gate",
    )(place, kept, taken, filters, lead_rows)


def weight_gradients(found, own, taken, val_pair, gain_row, rows):
    width = gain_row.shape[-1]
    channels = own.shape[-1]
    column = 512

    def body(*refs):
        blocks, (own, taken, val_own, val_core, gain, *kept, given, term) = refs[: Y + 1], refs[Y + 1 :]

        def rows_of(kind):
            parts = []
            for z in range(Z):
                for y in range(Y):
                    at = (2 * z + kind) * rows
                    if y < Y // 2:
                        parts.append(blocks[y][at : at + rows])
                    elif y > Y // 2:
                        parts.append(blocks[y + 1][at : at + rows])
                    else:
                        parts.append(blocks[y + z][kind * rows : (kind + 1) * rows])
            return jnp.concatenate(parts, axis=0)

        for kind in range(2):
            factor = jnp.concatenate(
                [ref[kind].reshape(Z * Y * rows, channels) for ref in (own, taken)], axis=1
            )
            grad = contract(factor, rows_of(kind), ((0,), (0,)))
            kept[kind][...] = grad[:channels]
            given[kind] = grad[channels:].astype(BF16)
            if kind == 0:
                total = jnp.sum(grad[:channels] * val_own[...].astype(F32), axis=0, keepdims=True)
                total += jnp.sum(grad[channels:] * val_core[...].astype(F32), axis=0, keepdims=True)
                term[...] = total / gain[...]

    operands = [found[y] for y in range(Y // 2)] + list(found[Y // 2]) + [found[y] for y in range(Y // 2 + 1, Y)]
    by_column = lambda count: pl.BlockSpec((count, column), lambda i: (0, i))
    whole = pl.BlockSpec(own.shape, lambda i: (0, 0, 0, 0))
    stacked = pl.BlockSpec((2, channels, column), lambda i: (0, 0, i))
    return pl.pallas_call(
        body,
        grid=(width // column,),
        in_specs=[by_column(o.shape[0]) for o in operands]
        + [whole, whole, by_column(channels), by_column(channels), by_column(1)],
        out_specs=[by_column(channels), by_column(channels), stacked, by_column(1)],
        out_shape=(
            jax.ShapeDtypeStruct((channels, width), F32),
            jax.ShapeDtypeStruct((channels, width), F32),
            jax.ShapeDtypeStruct((2, channels, width), BF16),
            jax.ShapeDtypeStruct((1, width), F32),
        ),
        compiler_params=vmem_params(24),
        cost_estimate=pl.CostEstimate(flops=1 << 30, bytes_accessed=13 << 20, transcendentals=0),
        name="weight_gradients",
    )(*operands, own, taken, *val_pair, gain_row)


def on_device(x_in, grad_out, gain, w_val, w_out, filt, tail, micro_index):
    x_rows, cot_rows, gain_row = x_in[0], grad_out[0], gain[0]
    val_weight, out_weight = w_val[0], w_out[0]
    filters, tail_rows = filt[0], tail[0]
    has_tail = micro_index[0] > 0
    rows, width = x_rows.shape
    channels = val_weight.shape[0]

    x_float = x_rows.astype(F32)
    inv_rms = lax.rsqrt(jnp.mean(x_float * x_float, axis=-1, keepdims=True) + EPSILON)
    normed = (x_float * inv_rms * gain_row).astype(BF16)

    own = jnp.concatenate([normed, cot_rows], axis=0)
    mate = lax.ppermute(own, "z", SWAP)
    found = gathered(jnp.concatenate([own, mate], axis=0))

    val_core = lax.ppermute(val_weight, "core", SWAP)
    out_core = lax.ppermute(out_weight, "core", SWAP)
    val_sent, _ = lax.optimization_barrier((val_weight, mate))
    val_z = lax.ppermute(val_sent, "z", SWAP)
    val_z_core = lax.ppermute(val_z, "core", SWAP)
    weights = lax.optimization_barrier(
        jnp.concatenate([val_weight, val_core, out_weight, out_core], axis=0)
    )

    def product(block):
        return contract(block, weights, ((1,), (1,)))

    products = [
        tuple(product(b) for b in found[y]) if y == Y // 2 else product(found[y]) for y in range(Y)
    ]
    kept, given = sorted_products(products, rows, channels)
    taken = lax.ppermute(given, "core", SWAP)
    val_z, val_z_core, kept = lax.optimization_barrier((val_z, val_z_core, kept))
    val_weights = jnp.concatenate([val_weight, val_core, val_z, val_z_core], axis=0)
    val_weights, kept = lax.optimization_barrier((val_weights, kept))

    place = jnp.stack([lax.axis_index(axis) for axis in TENSOR]).astype(jnp.int32)
    lead_rows = jnp.where(has_tail, tail_rows, jnp.zeros_like(tail_rows)).astype(F32)
    own, other, near_z, grad_filter, grad_lead = through_gate(place, kept, taken, filters, lead_rows)
    grad_tail = jnp.where(has_tail, grad_lead, jnp.zeros_like(grad_lead))

    taken = lax.ppermute(other, "core", SWAP)
    from_z = lax.ppermute(near_z[0], "z", SWAP)
    from_z_core = lax.ppermute(near_z[1], ("z", "core"), [(i, i ^ 3) for i in range(Z * CORE)])
    partial = weight_gradients(found, own, taken, (val_weight, val_core), gain_row[None], rows)
    from_z, from_z_core, partial = lax.optimization_barrier((from_z, from_z_core, partial))
    kept_val, kept_out, given, gain_term = partial

    share = contract(
        jnp.concatenate([own[0, 0], taken[0, 0], from_z, from_z_core], axis=1), val_weights, ((1,), (0,))
    )
    grad_normed, gain_term = reduced(share.astype(BF16).reshape(Y, rows, width), gain_term)
    taken = lax.ppermute(given, "core", SWAP)
    cot_late, taken = lax.optimization_barrier((cot_rows, taken))
    grad_wv = (kept_val + taken[0].astype(F32)).astype(BF16)
    grad_wo = (kept_out + taken[1].astype(F32)).astype(BF16)
    grad_gain = with_partner(gain_term, "y", 4)

    scaled = gain_row * grad_normed
    grad_local = (
        cot_late.astype(F32)
        + inv_rms * scaled
        - x_float * inv_rms**3 * jnp.mean(scaled * x_float, axis=-1, keepdims=True)
    )
    received = along(grad_local.astype(BF16), "section", -1)
    return (
        received[None],
        grad_wv[None],
        grad_wo[None],
        grad_filter[None],
        grad_tail[None],
        grad_gain,
    )


def solution(mesh):
    sections = mesh.shape["section"]
    split = Mesh(mesh.devices.reshape(sections, Y, Z, CORE), ("section", *TENSOR))
    by_rows = P("section", TENSOR, None)
    by_columns = P("section", None, TENSOR)
    whole = P("section", None)

    return jax.shard_map(
        on_device,
        mesh=split,
        in_specs=(by_rows, by_rows, whole, by_rows, by_rows, by_columns, by_columns, P("section")),
        out_specs=(by_rows, by_rows, by_rows, by_columns, by_columns, whole),
        check_vma=False,
    )
```

```python
import jax
import jax.numpy as jnp
from jax import lax
from jax.experimental import pallas as pl
from jax.experimental.pallas import tpu as pltpu
from jax.sharding import Mesh, PartitionSpec as P


TAPS = 3
EPSILON = 1e-06
Y, Z, CORE = 8, 2, 2
TENSOR = ("y", "z", "core")
SWAP = ((0, 1), (1, 0))
F32, BF16 = jnp.float32, jnp.bfloat16


def contract(left, right, dims):
    return lax.dot_general(left, right, (dims, ((), ())), preferred_element_type=F32)


def along(block, axis, distance):
    devices = lax.axis_size(axis)
    return lax.ppermute(block, axis, [(i, (i + distance) % devices) for i in range(devices)])


def with_partner(total, axis, apart):
    devices = range(lax.axis_size(axis))
    return total + lax.ppermute(total, axis, [(i, i ^ apart) for i in devices])


def gathered(own):
    half, rows = Y // 2, own.shape[0] // 2
    found = {0: own}
    ahead = behind = own
    for step in range(1, half):
        behind = along(behind, "y", 1)
        ahead = along(ahead, "y", -1)
        found[step], found[Y - step] = ahead, behind
    behind = along(behind[rows:], "y", 1)
    ahead = along(ahead[:rows], "y", -1)
    found[half] = (ahead, behind)
    return found


def reduced(share, total):
    found = {}

    def send(apart):
        found[apart] = along(share[apart], "y", apart)

    for apart in range(1, Y):
        send(apart)
    for axis, apart in (("core", 1), ("z", 1), ("y", 1), ("y", 2)):
        total = with_partner(total, axis, apart)
    grad_normed = share[0].astype(F32)
    for apart in range(1, Y):
        grad_normed = grad_normed + found[apart].astype(F32)
    return grad_normed, total


def vmem_params(mib):
    return pltpu.CompilerParams(vmem_limit_bytes=mib << 20)


def sorted_products(products, rows, channels):
    def body(*refs):
        kept, given = refs[-2:]
        for y in range(Y):
            for z in range(Z):
                for kind in range(2):
                    if y < Y // 2:
                        source, at = refs[y], (2 * z + kind) * rows
                    elif y > Y // 2:
                        source, at = refs[y + 1], (2 * z + kind) * rows
                    else:
                        source, at = refs[y + z], kind * rows
                    for core, target in enumerate((kept, given)):
                        column = (2 * kind + core) * channels
                        target[kind, z, y] = source[at : at + rows, column : column + channels]

    operands = [*products[: Y // 2], *products[Y // 2], *products[Y // 2 + 1 :]]
    shape = jax.ShapeDtypeStruct((2, Z, Y, rows, channels), F32)
    return pl.pallas_call(
        body,
        out_shape=(shape, shape),
        compiler_params=vmem_params(16),
        cost_estimate=pl.CostEstimate(flops=0, bytes_accessed=4 << 20, transcendentals=0),
        name="sorted_products",
    )(*operands)


def through_gate(place, kept, taken, filters, lead_rows):
    rows, channels = kept.shape[-2:]
    tokens = rows * Y * Z * CORE
    edge = 8

    def body(place, kept, taken, filters, lead, own, other, near_z, grad_filter, grad_lead, ext, cot, back, val, gat):
        def start(core, z, y):
            at_y = lax.rem(place[0] + y, Y)
            at_z = place[1] if z == 0 else 1 - place[1]
            at_core = place[2] if core == 0 else 1 - place[2]
            return pl.multiple_of(((at_y * Z + at_z) * CORE + at_core) * rows, rows)

        ext[0:edge] = jnp.zeros((edge, channels), F32)
        ext[edge - TAPS + 1 : edge] = lead[...]
        for core, source in enumerate((kept, taken)):
            for z in range(Z):
                for y in range(Y):
                    at = start(core, z, y)
                    ext[pl.ds(edge + at, rows)] = source[0, z, y].astype(BF16).astype(F32)
                    cot[pl.ds(at, rows)] = source[1, z, y]
        taps = [filters[k : k + 1, :] for k in range(TAPS)]
        delayed = [ext[edge - k : edge - k + tokens] for k in range(TAPS)]
        conv_out = taps[0] * delayed[0]
        for k in range(1, TAPS):
            conv_out = conv_out + taps[k] * delayed[k]
        gate_sig = jax.nn.sigmoid(conv_out)
        gat[...] = (conv_out * gate_sig).astype(BF16)
        grad_conv = cot[...] * gate_sig * (1.0 + conv_out * (1.0 - gate_sig))
        for k in range(TAPS):
            grad_filter[k : k + 1, :] = jnp.sum(grad_conv * delayed[k], axis=0, keepdims=True)
        back[0:edge] = jnp.zeros((edge, channels), F32)
        back[edge + tokens : edge + tokens + edge] = jnp.zeros((edge, channels), F32)
        back[edge : edge + tokens] = grad_conv
        grad_values = taps[0] * back[edge : edge + tokens]
        first = edge - TAPS + 1
        grad_head = taps[0] * back[first:edge]
        for k in range(1, TAPS):
            grad_values = grad_values + taps[k] * back[edge + k : edge + k + tokens]
            grad_head = grad_head + taps[k] * back[first + k : edge + k]
        grad_lead[...] = grad_head
        val[...] = grad_values.astype(BF16)
        for z in range(Z):
            for y in range(Y):
                block = slice(y * rows, (y + 1) * rows)
                at = start(0, z, y)
                own[0, z, block] = val[pl.ds(at, rows)]
                own[1, z, block] = gat[pl.ds(at, rows)]
                if z == 1:
                    near_z[0, block] = val[pl.ds(at, rows)]
                at = start(1, z, y)
                other[0, z, block] = val[pl.ds(at, rows)]
                other[1, z, block] = gat[pl.ds(at, rows)]
                if z == 1:
                    near_z[1, block] = val[pl.ds(at, rows)]

    vmem = pl.BlockSpec(memory_space=pltpu.VMEM)
    quarter = (Y * rows, channels)
    return pl.pallas_call(
        body,
        in_specs=[pl.BlockSpec(memory_space=pltpu.SMEM)] + [vmem] * 4,
        out_specs=[vmem] * 5,
        out_shape=(
            jax.ShapeDtypeStruct((2, Z, *quarter), BF16),
            jax.ShapeDtypeStruct((2, Z, *quarter), BF16),
            jax.ShapeDtypeStruct((CORE, *quarter), BF16),
            jax.ShapeDtypeStruct((TAPS, channels), F32),
            jax.ShapeDtypeStruct((TAPS - 1, channels), F32),
        ),
        scratch_shapes=[
            pltpu.VMEM((edge + tokens, channels), F32),
            pltpu.VMEM((tokens, channels), F32),
            pltpu.VMEM((edge + tokens + edge, channels), F32),
            pltpu.VMEM((tokens, channels), BF16),
            pltpu.VMEM((tokens, channels), BF16),
        ],
        compiler_params=vmem_params(16),
        cost_estimate=pl.CostEstimate(flops=4 << 20, bytes_accessed=4 << 20, transcendentals=1 << 16),
        name="through_gate",
    )(place, kept, taken, filters, lead_rows)


def weight_gradients(found, own, taken, val_pair, gain_row, rows):
    width = gain_row.shape[-1]
    channels = own.shape[-1]
    column = 512

    def body(*refs):
        blocks, (own, taken, val_own, val_core, gain, *kept, given, term) = refs[: Y + 1], refs[Y + 1 :]

        def rows_of(kind):
            parts = []
            for z in range(Z):
                for y in range(Y):
                    at = (2 * z + kind) * rows
                    if y < Y // 2:
                        parts.append(blocks[y][at : at + rows])
                    elif y > Y // 2:
                        parts.append(blocks[y + 1][at : at + rows])
                    else:
                        parts.append(blocks[y + z][kind * rows : (kind + 1) * rows])
            return jnp.concatenate(parts, axis=0)

        for kind in range(2):
            factor = jnp.concatenate(
                [ref[kind].reshape(Z * Y * rows, channels) for ref in (own, taken)], axis=1
            )
            grad = contract(factor, rows_of(kind), ((0,), (0,)))
            kept[kind][...] = grad[:channels]
            given[kind] = grad[channels:].astype(BF16)
            if kind == 0:
                total = jnp.sum(grad[:channels] * val_own[...].astype(F32), axis=0, keepdims=True)
                total += jnp.sum(grad[channels:] * val_core[...].astype(F32), axis=0, keepdims=True)
                term[...] = total / gain[...]

    operands = [found[y] for y in range(Y // 2)] + list(found[Y // 2]) + [found[y] for y in range(Y // 2 + 1, Y)]
    by_column = lambda count: pl.BlockSpec((count, column), lambda i: (0, i))
    whole = pl.BlockSpec(own.shape, lambda i: (0, 0, 0, 0))
    stacked = pl.BlockSpec((2, channels, column), lambda i: (0, 0, i))
    return pl.pallas_call(
        body,
        grid=(width // column,),
        in_specs=[by_column(o.shape[0]) for o in operands]
        + [whole, whole, by_column(channels), by_column(channels), by_column(1)],
        out_specs=[by_column(channels), by_column(channels), stacked, by_column(1)],
        out_shape=(
            jax.ShapeDtypeStruct((channels, width), F32),
            jax.ShapeDtypeStruct((channels, width), F32),
            jax.ShapeDtypeStruct((2, channels, width), BF16),
            jax.ShapeDtypeStruct((1, width), F32),
        ),
        compiler_params=vmem_params(24),
        cost_estimate=pl.CostEstimate(flops=1 << 30, bytes_accessed=13 << 20, transcendentals=0),
        name="weight_gradients",
    )(*operands, own, taken, *val_pair, gain_row)


def on_device(x_in, grad_out, gain, w_val, w_out, filt, tail, micro_index):
    x_rows, cot_rows, gain_row = x_in[0], grad_out[0], gain[0]
    val_weight, out_weight = w_val[0], w_out[0]
    filters, tail_rows = filt[0], tail[0]
    has_tail = micro_index[0] > 0
    rows, width = x_rows.shape
    channels = val_weight.shape[0]

    x_float = x_rows.astype(F32)
    inv_rms = lax.rsqrt(jnp.mean(x_float * x_float, axis=-1, keepdims=True) + EPSILON)
    normed = (x_float * inv_rms * gain_row).astype(BF16)

    own = jnp.concatenate([normed, cot_rows], axis=0)
    mate = lax.ppermute(own, "z", SWAP)
    found = gathered(jnp.concatenate([own, mate], axis=0))

    val_core = lax.ppermute(val_weight, "core", SWAP)
    out_core = lax.ppermute(out_weight, "core", SWAP)
    val_sent, _ = lax.optimization_barrier((val_weight, mate))
    val_z = lax.ppermute(val_sent, "z", SWAP)
    val_z_core = lax.ppermute(val_z, "core", SWAP)
    weights = lax.optimization_barrier(
        jnp.concatenate([val_weight, val_core, out_weight, out_core], axis=0)
    )

    def product(block):
        return contract(block, weights, ((1,), (1,)))

    products = [
        tuple(product(b) for b in found[y]) if y == Y // 2 else product(found[y]) for y in range(Y)
    ]
    kept, given = sorted_products(products, rows, channels)
    taken = lax.ppermute(given, "core", SWAP)
    val_z, val_z_core, kept = lax.optimization_barrier((val_z, val_z_core, kept))
    val_weights = jnp.concatenate([val_weight, val_core, val_z, val_z_core], axis=0)
    val_weights, kept = lax.optimization_barrier((val_weights, kept))

    place = jnp.stack([lax.axis_index(axis) for axis in TENSOR]).astype(jnp.int32)
    lead_rows = jnp.where(has_tail, tail_rows, jnp.zeros_like(tail_rows)).astype(F32)
    own, other, near_z, grad_filter, grad_lead = through_gate(place, kept, taken, filters, lead_rows)
    grad_tail = jnp.where(has_tail, grad_lead, jnp.zeros_like(grad_lead))

    taken = lax.ppermute(other, "core", SWAP)
    from_z = lax.ppermute(near_z[0], "z", SWAP)
    from_z_core = lax.ppermute(near_z[1], ("z", "core"), [(i, i ^ 3) for i in range(Z * CORE)])
    partial = weight_gradients(found, own, taken, (val_weight, val_core), gain_row[None], rows)
    from_z, from_z_core, partial = lax.optimization_barrier((from_z, from_z_core, partial))
    kept_val, kept_out, given, gain_term = partial

    share = contract(
        jnp.concatenate([own[0, 0], taken[0, 0], from_z, from_z_core], axis=1), val_weights, ((1,), (0,))
    )
    grad_normed, gain_term = reduced(share.astype(BF16).reshape(Y, rows, width), gain_term)
    taken = lax.ppermute(given, "core", SWAP)
    cot_late, taken = lax.optimization_barrier((cot_rows, taken))
    grad_wv = (kept_val + taken[0].astype(F32)).astype(BF16)
    grad_wo = (kept_out + taken[1].astype(F32)).astype(BF16)
    gain_other = lax.ppermute(gain_term, "y", [(i, i ^ 4) for i in range(Y)])

    scaled = gain_row * grad_normed
    grad_local = (
        cot_late.astype(F32)
        + inv_rms * scaled
        - x_float * inv_rms**3 * jnp.mean(scaled * x_float, axis=-1, keepdims=True)
    )
    grad_local = grad_local.astype(BF16)
    received = along(grad_local, "section", -1)
    gain_other, grad_wv, grad_wo, _ = lax.optimization_barrier((gain_other, grad_wv, grad_wo, grad_local))
    grad_gain = gain_term + gain_other
    return (
        received[None],
        grad_wv[None],
        grad_wo[None],
        grad_filter[None],
        grad_tail[None],
        grad_gain,
    )


def solution(mesh):
    sections = mesh.shape["section"]
    split = Mesh(mesh.devices.reshape(sections, Y, Z, CORE), ("section", *TENSOR))
    by_rows = P("section", TENSOR, None)
    by_columns = P("section", None, TENSOR)
    whole = P("section", None)

    return jax.shard_map(
        on_device,
        mesh=split,
        in_specs=(by_rows, by_rows, whole, by_rows, by_rows, by_columns, by_columns, P("section")),
        out_specs=(by_rows, by_rows, by_rows, by_columns, by_columns, whole),
        check_vma=False,
    )
```

```python
import jax
import jax.numpy as jnp
from jax import lax
from jax.experimental import pallas as pl
from jax.experimental.pallas import tpu as pltpu
from jax.sharding import Mesh, PartitionSpec as P


TAPS = 3
EPSILON = 1e-06
Y, Z, CORE = 8, 2, 2
TENSOR = ("y", "z", "core")
SWAP = ((0, 1), (1, 0))
F32, BF16 = jnp.float32, jnp.bfloat16


def contract(left, right, dims):
    return lax.dot_general(left, right, (dims, ((), ())), preferred_element_type=F32)


def along(block, axis, distance):
    devices = lax.axis_size(axis)
    return lax.ppermute(block, axis, [(i, (i + distance) % devices) for i in range(devices)])


def with_partner(total, axis, apart):
    devices = range(lax.axis_size(axis))
    return total + lax.ppermute(total, axis, [(i, i ^ apart) for i in devices])


def gathered(own):
    half, rows = Y // 2, own.shape[0] // 2
    found = {0: own}
    ahead = behind = own
    for step in range(1, half):
        behind = along(behind, "y", 1)
        ahead = along(ahead, "y", -1)
        found[step], found[Y - step] = ahead, behind
    behind = along(behind[rows:], "y", 1)
    ahead = along(ahead[:rows], "y", -1)
    found[half] = (ahead, behind)
    return found


def vmem_params(mib):
    return pltpu.CompilerParams(vmem_limit_bytes=mib << 20)


def sorted_products(products, rows, channels):
    def body(*refs):
        kept, given = refs[-2:]
        for y in range(Y):
            for z in range(Z):
                for kind in range(2):
                    if y < Y // 2:
                        source, at = refs[y], (2 * z + kind) * rows
                    elif y > Y // 2:
                        source, at = refs[y + 1], (2 * z + kind) * rows
                    else:
                        source, at = refs[y + z], kind * rows
                    for core, target in enumerate((kept, given)):
                        column = (2 * kind + core) * channels
                        target[kind, z, y] = source[at : at + rows, column : column + channels]

    operands = [*products[: Y // 2], *products[Y // 2], *products[Y // 2 + 1 :]]
    shape = jax.ShapeDtypeStruct((2, Z, Y, rows, channels), F32)
    return pl.pallas_call(
        body,
        out_shape=(shape, shape),
        compiler_params=vmem_params(16),
        cost_estimate=pl.CostEstimate(flops=0, bytes_accessed=4 << 20, transcendentals=0),
        name="sorted_products",
    )(*operands)


def through_gate(place, kept, taken, filters, lead_rows):
    rows, channels = kept.shape[-2:]
    tokens = rows * Y * Z * CORE
    edge = 8

    def body(place, kept, taken, filters, lead, own, other, near_z, grad_filter, grad_lead, ext, cot, back, val, gat):
        def start(core, z, y):
            at_y = lax.rem(place[0] + y, Y)
            at_z = place[1] if z == 0 else 1 - place[1]
            at_core = place[2] if core == 0 else 1 - place[2]
            return pl.multiple_of(((at_y * Z + at_z) * CORE + at_core) * rows, rows)

        ext[0:edge] = jnp.zeros((edge, channels), F32)
        ext[edge - TAPS + 1 : edge] = lead[...]
        for core, source in enumerate((kept, taken)):
            for z in range(Z):
                for y in range(Y):
                    at = start(core, z, y)
                    ext[pl.ds(edge + at, rows)] = source[0, z, y].astype(BF16).astype(F32)
                    cot[pl.ds(at, rows)] = source[1, z, y]
        taps = [filters[k : k + 1, :] for k in range(TAPS)]
        delayed = [ext[edge - k : edge - k + tokens] for k in range(TAPS)]
        conv_out = taps[0] * delayed[0]
        for k in range(1, TAPS):
            conv_out = conv_out + taps[k] * delayed[k]
        gate_sig = jax.nn.sigmoid(conv_out)
        gat[...] = (conv_out * gate_sig).astype(BF16)
        grad_conv = cot[...] * gate_sig * (1.0 + conv_out * (1.0 - gate_sig))
        for k in range(TAPS):
            grad_filter[k : k + 1, :] = jnp.sum(grad_conv * delayed[k], axis=0, keepdims=True)
        back[0:edge] = jnp.zeros((edge, channels), F32)
        back[edge + tokens : edge + tokens + edge] = jnp.zeros((edge, channels), F32)
        back[edge : edge + tokens] = grad_conv
        grad_values = taps[0] * back[edge : edge + tokens]
        first = edge - TAPS + 1
        grad_head = taps[0] * back[first:edge]
        for k in range(1, TAPS):
            grad_values = grad_values + taps[k] * back[edge + k : edge + k + tokens]
            grad_head = grad_head + taps[k] * back[first + k : edge + k]
        grad_lead[...] = grad_head
        val[...] = grad_values.astype(BF16)
        for z in range(Z):
            for y in range(Y):
                block = slice(y * rows, (y + 1) * rows)
                at = start(0, z, y)
                own[0, z, block] = val[pl.ds(at, rows)]
                own[1, z, block] = gat[pl.ds(at, rows)]
                if z == 1:
                    near_z[0, block] = val[pl.ds(at, rows)]
                at = start(1, z, y)
                other[0, z, block] = val[pl.ds(at, rows)]
                other[1, z, block] = gat[pl.ds(at, rows)]
                if z == 1:
                    near_z[1, block] = val[pl.ds(at, rows)]

    vmem = pl.BlockSpec(memory_space=pltpu.VMEM)
    quarter = (Y * rows, channels)
    return pl.pallas_call(
        body,
        in_specs=[pl.BlockSpec(memory_space=pltpu.SMEM)] + [vmem] * 4,
        out_specs=[vmem] * 5,
        out_shape=(
            jax.ShapeDtypeStruct((2, Z, *quarter), BF16),
            jax.ShapeDtypeStruct((2, Z, *quarter), BF16),
            jax.ShapeDtypeStruct((CORE, *quarter), BF16),
            jax.ShapeDtypeStruct((TAPS, channels), F32),
            jax.ShapeDtypeStruct((TAPS - 1, channels), F32),
        ),
        scratch_shapes=[
            pltpu.VMEM((edge + tokens, channels), F32),
            pltpu.VMEM((tokens, channels), F32),
            pltpu.VMEM((edge + tokens + edge, channels), F32),
            pltpu.VMEM((tokens, channels), BF16),
            pltpu.VMEM((tokens, channels), BF16),
        ],
        compiler_params=vmem_params(16),
        cost_estimate=pl.CostEstimate(flops=4 << 20, bytes_accessed=4 << 20, transcendentals=1 << 16),
        name="through_gate",
    )(place, kept, taken, filters, lead_rows)


def weight_gradients(found, own, taken, val_pair, gain_row, rows):
    width = gain_row.shape[-1]
    channels = own.shape[-1]
    column = 512

    def body(*refs):
        blocks, (own, taken, val_own, val_core, gain, *kept, given, term) = refs[: Y + 1], refs[Y + 1 :]

        def rows_of(kind):
            parts = []
            for z in range(Z):
                for y in range(Y):
                    at = (2 * z + kind) * rows
                    if y < Y // 2:
                        parts.append(blocks[y][at : at + rows])
                    elif y > Y // 2:
                        parts.append(blocks[y + 1][at : at + rows])
                    else:
                        parts.append(blocks[y + z][kind * rows : (kind + 1) * rows])
            return jnp.concatenate(parts, axis=0)

        for kind in range(2):
            factor = jnp.concatenate(
                [ref[kind].reshape(Z * Y * rows, channels) for ref in (own, taken)], axis=1
            )
            grad = contract(factor, rows_of(kind), ((0,), (0,)))
            kept[kind][...] = grad[:channels]
            given[kind] = grad[channels:].astype(BF16)
            if kind == 0:
                total = jnp.sum(grad[:channels] * val_own[...].astype(F32), axis=0, keepdims=True)
                total += jnp.sum(grad[channels:] * val_core[...].astype(F32), axis=0, keepdims=True)
                term[...] = total / gain[...]

    operands = [found[y] for y in range(Y // 2)] + list(found[Y // 2]) + [found[y] for y in range(Y // 2 + 1, Y)]
    by_column = lambda count: pl.BlockSpec((count, column), lambda i: (0, i))
    whole = pl.BlockSpec(own.shape, lambda i: (0, 0, 0, 0))
    stacked = pl.BlockSpec((2, channels, column), lambda i: (0, 0, i))
    return pl.pallas_call(
        body,
        grid=(width // column,),
        in_specs=[by_column(o.shape[0]) for o in operands]
        + [whole, whole, by_column(channels), by_column(channels), by_column(1)],
        out_specs=[by_column(channels), by_column(channels), stacked, by_column(1)],
        out_shape=(
            jax.ShapeDtypeStruct((channels, width), F32),
            jax.ShapeDtypeStruct((channels, width), F32),
            jax.ShapeDtypeStruct((2, channels, width), BF16),
            jax.ShapeDtypeStruct((1, width), F32),
        ),
        compiler_params=vmem_params(24),
        cost_estimate=pl.CostEstimate(flops=1 << 30, bytes_accessed=13 << 20, transcendentals=0),
        name="weight_gradients",
    )(*operands, own, taken, *val_pair, gain_row)


def shares(factors, weights, total, rows):
    width = total.shape[-1]
    side = width // rows
    column = 512

    def body(*refs):
        factors, weights, total, messages, square = refs[:4], refs[4:8], refs[8], refs[9:-1], refs[-1]
        left = [ref[...] for ref in factors]
        for at in range(0, width, column):
            share = contract(left[0], weights[0][:, at : at + column], ((1,), (0,)))
            for i in range(1, 4):
                share += contract(left[i], weights[i][:, at : at + column], ((1,), (0,)))
            share = share.astype(BF16)
            for y in range(Y):
                messages[y][:, at : at + column] = share[y * rows : (y + 1) * rows]
        for row in range(rows):
            square[row : row + 1, :] = total[:, row * side : (row + 1) * side]
        first = square[...].astype(BF16)
        second = (square[...] - first.astype(F32)).astype(BF16)
        for y in range(Y):
            messages[y][:, width : width + side] = first
            messages[y][:, width + side :] = second

    return pl.pallas_call(
        body,
        out_shape=[jax.ShapeDtypeStruct((rows, width + 2 * side), BF16)] * Y,
        scratch_shapes=[pltpu.VMEM((rows, side), F32)],
        compiler_params=vmem_params(16),
        cost_estimate=pl.CostEstimate(flops=1 << 29, bytes_accessed=6 << 20, transcendentals=0),
        name="shares",
    )(*factors, *weights, total)


def ended(place, messages, x_rows, cot_rows, gain_row, inv_rms):
    rows, width = x_rows.shape
    side = (messages[0].shape[1] - width) // 2

    def body(place, *refs):
        messages, (x_rows, cot_rows, gain, inv_rms, grad_local, total, terms) = refs[:Y], refs[Y:]
        grad_normed = messages[0][:, :width].astype(F32)
        for back in range(1, Y):
            grad_normed = grad_normed + messages[back][:, :width].astype(F32)
        for back in range(Y):
            sender = lax.rem(place[0] + (Y - back), Y)
            first = messages[back][:, width : width + side].astype(F32)
            terms[sender] = first + messages[back][:, width + side :].astype(F32)
        added = terms[0]
        for y in range(1, Y):
            added = added + terms[y]
        total[...] = added
        x_float = x_rows[...].astype(F32)
        inv = inv_rms[...]
        scaled = gain[...] * grad_normed
        mean = jnp.sum(scaled * x_float, axis=-1, keepdims=True) / width
        grad_local[...] = (cot_rows[...].astype(F32) + inv * scaled - x_float * (inv * inv * inv * mean)).astype(BF16)

    vmem = pl.BlockSpec(memory_space=pltpu.VMEM)
    return pl.pallas_call(
        body,
        in_specs=[pl.BlockSpec(memory_space=pltpu.SMEM)] + [vmem] * (Y + 4),
        out_specs=[vmem, vmem],
        out_shape=(jax.ShapeDtypeStruct((rows, width), BF16), jax.ShapeDtypeStruct((rows, side), F32)),
        scratch_shapes=[pltpu.VMEM((Y, rows, side), F32)],
        compiler_params=vmem_params(16),
        cost_estimate=pl.CostEstimate(flops=2 << 20, bytes_accessed=2 << 20, transcendentals=0),
        name="ended",
    )(place, *messages, x_rows, cot_rows, gain_row, inv_rms)


def on_device(x_in, grad_out, gain, w_val, w_out, filt, tail, micro_index):
    x_rows, cot_rows, gain_row = x_in[0], grad_out[0], gain[0]
    val_weight, out_weight = w_val[0], w_out[0]
    filters, tail_rows = filt[0], tail[0]
    has_tail = micro_index[0] > 0
    rows, width = x_rows.shape
    channels = val_weight.shape[0]

    x_float = x_rows.astype(F32)
    inv_rms = lax.rsqrt(jnp.mean(x_float * x_float, axis=-1, keepdims=True) + EPSILON)
    normed = (x_float * inv_rms * gain_row).astype(BF16)

    own = jnp.concatenate([normed, cot_rows], axis=0)
    mate = lax.ppermute(own, "z", SWAP)
    found = gathered(jnp.concatenate([own, mate], axis=0))

    val_core = lax.ppermute(val_weight, "core", SWAP)
    out_core = lax.ppermute(out_weight, "core", SWAP)
    val_sent, _ = lax.optimization_barrier((val_weight, mate))
    val_z = lax.ppermute(val_sent, "z", SWAP)
    val_z_core = lax.ppermute(val_z, "core", SWAP)
    weights = lax.optimization_barrier(
        jnp.concatenate([val_weight, val_core, out_weight, out_core], axis=0)
    )

    def product(block):
        return contract(block, weights, ((1,), (1,)))

    products = [
        tuple(product(b) for b in found[y]) if y == Y // 2 else product(found[y]) for y in range(Y)
    ]
    kept, given = sorted_products(products, rows, channels)
    taken = lax.ppermute(given, "core", SWAP)
    val_z, val_z_core, kept = lax.optimization_barrier((val_z, val_z_core, kept))

    place = jnp.stack([lax.axis_index(axis) for axis in TENSOR]).astype(jnp.int32)
    lead_rows = jnp.where(has_tail, tail_rows, jnp.zeros_like(tail_rows)).astype(F32)
    own, other, near_z, grad_filter, grad_lead = through_gate(place, kept, taken, filters, lead_rows)
    grad_tail = jnp.where(has_tail, grad_lead, jnp.zeros_like(grad_lead))

    taken = lax.ppermute(other, "core", SWAP)
    from_z = lax.ppermute(near_z[0], "z", SWAP)
    from_z_core = lax.ppermute(near_z[1], ("z", "core"), [(i, i ^ 3) for i in range(Z * CORE)])
    partial = weight_gradients(found, own, taken, (val_weight, val_core), gain_row[None], rows)
    from_z, from_z_core, partial = lax.optimization_barrier((from_z, from_z_core, partial))
    kept_val, kept_out, given, gain_term = partial

    messages = shares(
        (own[0, 0], taken[0, 0], from_z, from_z_core), (val_weight, val_core, val_z, val_z_core), gain_term, rows
    )
    arrived = [messages[0]]
    for apart in range(1, Y):
        arrived.append(along(messages[apart], "y", apart))
    taken = lax.ppermute(given, "core", SWAP)
    arrived, taken = lax.optimization_barrier((arrived, taken))
    grad_local, gain_term = ended(place, arrived, x_rows, cot_rows, gain_row[None], inv_rms)
    received = along(grad_local, "section", -1)
    gain_term = with_partner(gain_term, "z", 1)
    grad_gain = with_partner(gain_term, "core", 1).reshape(1, width)
    taken, grad_local = lax.optimization_barrier((taken, grad_local))
    grad_wv = (kept_val + taken[0].astype(F32)).astype(BF16)
    grad_wo = (kept_out + taken[1].astype(F32)).astype(BF16)
    return (
        received[None],
        grad_wv[None],
        grad_wo[None],
        grad_filter[None],
        grad_tail[None],
        grad_gain,
    )


def solution(mesh):
    sections = mesh.shape["section"]
    split = Mesh(mesh.devices.reshape(sections, Y, Z, CORE), ("section", *TENSOR))
    by_rows = P("section", TENSOR, None)
    by_columns = P("section", None, TENSOR)
    whole = P("section", None)

    return jax.shard_map(
        on_device,
        mesh=split,
        in_specs=(by_rows, by_rows, whole, by_rows, by_rows, by_columns, by_columns, P("section")),
        out_specs=(by_rows, by_rows, by_rows, by_columns, by_columns, whole),
        check_vma=False,
    )
```

```python
import jax
import jax.numpy as jnp
from jax import lax
from jax.experimental import pallas as pl
from jax.experimental.pallas import tpu as pltpu
from jax.sharding import Mesh, PartitionSpec as P


TAPS = 3
EPSILON = 1e-06
Y, Z, CORE = 8, 2, 2
TENSOR = ("y", "z", "core")
SWAP = ((0, 1), (1, 0))
F32, BF16 = jnp.float32, jnp.bfloat16


def contract(left, right, dims):
    return lax.dot_general(left, right, (dims, ((), ())), preferred_element_type=F32)


def along(block, axis, distance):
    devices = lax.axis_size(axis)
    return lax.ppermute(block, axis, [(i, (i + distance) % devices) for i in range(devices)])


def with_partner(total, axis, apart):
    devices = range(lax.axis_size(axis))
    return total + lax.ppermute(total, axis, [(i, i ^ apart) for i in devices])


def gathered(own):
    half, rows = Y // 2, own.shape[0] // 2
    found = {0: own}
    ahead = behind = own
    for step in range(1, half):
        behind = along(behind, "y", 1)
        ahead = along(ahead, "y", -1)
        found[step], found[Y - step] = ahead, behind
    behind = along(behind[rows:], "y", 1)
    ahead = along(ahead[:rows], "y", -1)
    found[half] = (ahead, behind)
    return found


def vmem_params(mib):
    return pltpu.CompilerParams(vmem_limit_bytes=mib << 20)


def sorted_products(products, rows, channels):
    def body(*refs):
        kept, given = refs[-2:]
        for y in range(Y):
            for z in range(Z):
                for kind in range(2):
                    if y < Y // 2:
                        source, at = refs[y], (2 * z + kind) * rows
                    elif y > Y // 2:
                        source, at = refs[y + 1], (2 * z + kind) * rows
                    else:
                        source, at = refs[y + z], kind * rows
                    for core, target in enumerate((kept, given)):
                        column = (2 * kind + core) * channels
                        target[kind, z, y] = source[at : at + rows, column : column + channels]

    operands = [*products[: Y // 2], *products[Y // 2], *products[Y // 2 + 1 :]]
    shape = jax.ShapeDtypeStruct((2, Z, Y, rows, channels), F32)
    return pl.pallas_call(
        body,
        out_shape=(shape, shape),
        compiler_params=vmem_params(16),
        cost_estimate=pl.CostEstimate(flops=0, bytes_accessed=4 << 20, transcendentals=0),
        name="sorted_products",
    )(*operands)


def through_gate(place, kept, taken, filters, lead_rows):
    rows, channels = kept.shape[-2:]
    tokens = rows * Y * Z * CORE
    edge = 8

    def body(place, kept, taken, filters, lead, own, other, near_z, grad_filter, grad_lead, ext, cot, back, val, gat):
        def start(core, z, y):
            at_y = lax.rem(place[0] + y, Y)
            at_z = place[1] if z == 0 else 1 - place[1]
            at_core = place[2] if core == 0 else 1 - place[2]
            return pl.multiple_of(((at_y * Z + at_z) * CORE + at_core) * rows, rows)

        ext[0:edge] = jnp.zeros((edge, channels), F32)
        ext[edge - TAPS + 1 : edge] = lead[...]
        for core, source in enumerate((kept, taken)):
            for z in range(Z):
                for y in range(Y):
                    at = start(core, z, y)
                    ext[pl.ds(edge + at, rows)] = source[0, z, y].astype(BF16).astype(F32)
                    cot[pl.ds(at, rows)] = source[1, z, y]
        taps = [filters[k : k + 1, :] for k in range(TAPS)]
        delayed = [ext[edge - k : edge - k + tokens] for k in range(TAPS)]
        conv_out = taps[0] * delayed[0]
        for k in range(1, TAPS):
            conv_out = conv_out + taps[k] * delayed[k]
        gate_sig = jax.nn.sigmoid(conv_out)
        gat[...] = (conv_out * gate_sig).astype(BF16)
        grad_conv = cot[...] * gate_sig * (1.0 + conv_out * (1.0 - gate_sig))
        for k in range(TAPS):
            grad_filter[k : k + 1, :] = jnp.sum(grad_conv * delayed[k], axis=0, keepdims=True)
        back[0:edge] = jnp.zeros((edge, channels), F32)
        back[edge + tokens : edge + tokens + edge] = jnp.zeros((edge, channels), F32)
        back[edge : edge + tokens] = grad_conv
        grad_values = taps[0] * back[edge : edge + tokens]
        first = edge - TAPS + 1
        grad_head = taps[0] * back[first:edge]
        for k in range(1, TAPS):
            grad_values = grad_values + taps[k] * back[edge + k : edge + k + tokens]
            grad_head = grad_head + taps[k] * back[first + k : edge + k]
        grad_lead[...] = grad_head
        val[...] = grad_values.astype(BF16)
        for z in range(Z):
            for y in range(Y):
                block = slice(y * rows, (y + 1) * rows)
                at = start(0, z, y)
                own[0, z, block] = val[pl.ds(at, rows)]
                own[1, z, block] = gat[pl.ds(at, rows)]
                if z == 1:
                    near_z[0, block] = val[pl.ds(at, rows)]
                at = start(1, z, y)
                other[0, z, block] = val[pl.ds(at, rows)]
                other[1, z, block] = gat[pl.ds(at, rows)]
                if z == 1:
                    near_z[1, block] = val[pl.ds(at, rows)]

    vmem = pl.BlockSpec(memory_space=pltpu.VMEM)
    quarter = (Y * rows, channels)
    return pl.pallas_call(
        body,
        in_specs=[pl.BlockSpec(memory_space=pltpu.SMEM)] + [vmem] * 4,
        out_specs=[vmem] * 5,
        out_shape=(
            jax.ShapeDtypeStruct((2, Z, *quarter), BF16),
            jax.ShapeDtypeStruct((2, Z, *quarter), BF16),
            jax.ShapeDtypeStruct((CORE, *quarter), BF16),
            jax.ShapeDtypeStruct((TAPS, channels), F32),
            jax.ShapeDtypeStruct((TAPS - 1, channels), F32),
        ),
        scratch_shapes=[
            pltpu.VMEM((edge + tokens, channels), F32),
            pltpu.VMEM((tokens, channels), F32),
            pltpu.VMEM((edge + tokens + edge, channels), F32),
            pltpu.VMEM((tokens, channels), BF16),
            pltpu.VMEM((tokens, channels), BF16),
        ],
        compiler_params=vmem_params(16),
        cost_estimate=pl.CostEstimate(flops=4 << 20, bytes_accessed=4 << 20, transcendentals=1 << 16),
        name="through_gate",
    )(place, kept, taken, filters, lead_rows)


def weight_gradients(found, own, taken, val_pair, gain_row, rows):
    width = gain_row.shape[-1]
    channels = own.shape[-1]
    column = 512

    def body(*refs):
        blocks, (own, taken, val_own, val_core, gain, *kept, given, term) = refs[: Y + 1], refs[Y + 1 :]

        def rows_of(kind):
            parts = []
            for z in range(Z):
                for y in range(Y):
                    at = (2 * z + kind) * rows
                    if y < Y // 2:
                        parts.append(blocks[y][at : at + rows])
                    elif y > Y // 2:
                        parts.append(blocks[y + 1][at : at + rows])
                    else:
                        parts.append(blocks[y + z][kind * rows : (kind + 1) * rows])
            return jnp.concatenate(parts, axis=0)

        for kind in range(2):
            factor = jnp.concatenate(
                [ref[kind].reshape(Z * Y * rows, channels) for ref in (own, taken)], axis=1
            )
            grad = contract(factor, rows_of(kind), ((0,), (0,)))
            kept[kind][...] = grad[:channels]
            given[kind] = grad[channels:].astype(BF16)
            if kind == 0:
                total = jnp.sum(grad[:channels] * val_own[...].astype(F32), axis=0, keepdims=True)
                total += jnp.sum(grad[channels:] * val_core[...].astype(F32), axis=0, keepdims=True)
                term[...] = total / gain[...]

    operands = [found[y] for y in range(Y // 2)] + list(found[Y // 2]) + [found[y] for y in range(Y // 2 + 1, Y)]
    by_column = lambda count: pl.BlockSpec((count, column), lambda i: (0, i))
    whole = pl.BlockSpec(own.shape, lambda i: (0, 0, 0, 0))
    stacked = pl.BlockSpec((2, channels, column), lambda i: (0, 0, i))
    return pl.pallas_call(
        body,
        grid=(width // column,),
        in_specs=[by_column(o.shape[0]) for o in operands]
        + [whole, whole, by_column(channels), by_column(channels), by_column(1)],
        out_specs=[by_column(channels), by_column(channels), stacked, by_column(1)],
        out_shape=(
            jax.ShapeDtypeStruct((channels, width), F32),
            jax.ShapeDtypeStruct((channels, width), F32),
            jax.ShapeDtypeStruct((2, channels, width), BF16),
            jax.ShapeDtypeStruct((1, width), F32),
        ),
        compiler_params=vmem_params(24),
        cost_estimate=pl.CostEstimate(flops=1 << 30, bytes_accessed=13 << 20, transcendentals=0),
        name="weight_gradients",
    )(*operands, own, taken, *val_pair, gain_row)


def shares(factors, weights, total, rows):
    width = total.shape[-1]
    side = width // rows
    column = 512

    def body(*refs):
        factors, weights, total, messages, square = refs[:4], refs[4:8], refs[8], refs[9:-1], refs[-1]
        left = [ref[...] for ref in factors]
        for at in range(0, width, column):
            share = contract(left[0], weights[0][:, at : at + column], ((1,), (0,)))
            for i in range(1, 4):
                share += contract(left[i], weights[i][:, at : at + column], ((1,), (0,)))
            share = share.astype(BF16)
            for y in range(Y):
                messages[y][:, at : at + column] = share[y * rows : (y + 1) * rows]
        for row in range(rows):
            square[row : row + 1, :] = total[:, row * side : (row + 1) * side]
        first = square[...].astype(BF16)
        second = (square[...] - first.astype(F32)).astype(BF16)
        for y in range(Y):
            messages[y][:, width : width + side] = first
            messages[y][:, width + side :] = second

    return pl.pallas_call(
        body,
        out_shape=[jax.ShapeDtypeStruct((rows, width + 2 * side), BF16)] * Y,
        scratch_shapes=[pltpu.VMEM((rows, side), F32)],
        compiler_params=vmem_params(16),
        cost_estimate=pl.CostEstimate(flops=1 << 29, bytes_accessed=6 << 20, transcendentals=0),
        name="shares",
    )(*factors, *weights, total)


def ended(place, messages, x_rows, cot_rows, gain_row, inv_rms):
    rows, width = x_rows.shape
    side = (messages[0].shape[1] - width) // 2

    def body(place, *refs):
        messages, (x_rows, cot_rows, gain, inv_rms, grad_local, total, terms) = refs[:Y], refs[Y:]
        grad_normed = messages[0][:, :width].astype(F32)
        for back in range(1, Y):
            grad_normed = grad_normed + messages[back][:, :width].astype(F32)
        for back in range(Y):
            sender = lax.rem(place[0] + (Y - back), Y)
            first = messages[back][:, width : width + side].astype(F32)
            terms[sender] = first + messages[back][:, width + side :].astype(F32)
        added = terms[0]
        for y in range(1, Y):
            added = added + terms[y]
        total[...] = added
        x_float = x_rows[...].astype(F32)
        inv = inv_rms[...]
        scaled = gain[...] * grad_normed
        mean = jnp.sum(scaled * x_float, axis=-1, keepdims=True) / width
        grad_local[...] = (cot_rows[...].astype(F32) + inv * scaled - x_float * (inv * inv * inv * mean)).astype(BF16)

    vmem = pl.BlockSpec(memory_space=pltpu.VMEM)
    return pl.pallas_call(
        body,
        in_specs=[pl.BlockSpec(memory_space=pltpu.SMEM)] + [vmem] * (Y + 4),
        out_specs=[vmem, vmem],
        out_shape=(jax.ShapeDtypeStruct((rows, width), BF16), jax.ShapeDtypeStruct((rows, side), F32)),
        scratch_shapes=[pltpu.VMEM((Y, rows, side), F32)],
        compiler_params=vmem_params(16),
        cost_estimate=pl.CostEstimate(flops=2 << 20, bytes_accessed=2 << 20, transcendentals=0),
        name="ended",
    )(place, *messages, x_rows, cot_rows, gain_row, inv_rms)


def on_device(x_in, grad_out, gain, w_val, w_out, filt, tail, micro_index):
    x_rows, cot_rows, gain_row = x_in[0], grad_out[0], gain[0]
    val_weight, out_weight = w_val[0], w_out[0]
    filters, tail_rows = filt[0], tail[0]
    has_tail = micro_index[0] > 0
    rows, width = x_rows.shape
    channels = val_weight.shape[0]

    x_float = x_rows.astype(F32)
    inv_rms = lax.rsqrt(jnp.mean(x_float * x_float, axis=-1, keepdims=True) + EPSILON)
    normed = (x_float * inv_rms * gain_row).astype(BF16)

    own = jnp.concatenate([normed, cot_rows], axis=0)
    mate = lax.ppermute(own, "z", SWAP)
    found = gathered(jnp.concatenate([own, mate], axis=0))

    val_core = lax.ppermute(val_weight, "core", SWAP)
    out_core = lax.ppermute(out_weight, "core", SWAP)
    val_sent, _ = lax.optimization_barrier((val_weight, mate))
    val_z = lax.ppermute(val_sent, "z", SWAP)
    val_z_core = lax.ppermute(val_z, "core", SWAP)
    weights = lax.optimization_barrier(
        jnp.concatenate([val_weight, val_core, out_weight, out_core], axis=0)
    )

    def product(block):
        return contract(block, weights, ((1,), (1,)))

    products = [
        tuple(product(b) for b in found[y]) if y == Y // 2 else product(found[y]) for y in range(Y)
    ]
    kept, given = sorted_products(products, rows, channels)
    taken = lax.ppermute(given, "core", SWAP)
    val_z, val_z_core, kept = lax.optimization_barrier((val_z, val_z_core, kept))

    place = jnp.stack([lax.axis_index(axis) for axis in TENSOR]).astype(jnp.int32)
    lead_rows = jnp.where(has_tail, tail_rows, jnp.zeros_like(tail_rows)).astype(F32)
    own, other, near_z, grad_filter, grad_lead = through_gate(place, kept, taken, filters, lead_rows)
    grad_tail = jnp.where(has_tail, grad_lead, jnp.zeros_like(grad_lead))

    taken = lax.ppermute(other, "core", SWAP)
    from_z = lax.ppermute(near_z[0], "z", SWAP)
    from_z_core = lax.ppermute(near_z[1], ("z", "core"), [(i, i ^ 3) for i in range(Z * CORE)])
    partial = weight_gradients(found, own, taken, (val_weight, val_core), gain_row[None], rows)
    from_z, from_z_core, partial = lax.optimization_barrier((from_z, from_z_core, partial))
    kept_val, kept_out, given, gain_term = partial
    swapped = lax.ppermute(given, "core", SWAP)

    messages = shares(
        (own[0, 0], taken[0, 0], from_z, from_z_core), (val_weight, val_core, val_z, val_z_core), gain_term, rows
    )
    arrived = [messages[0]]
    for apart in range(1, Y):
        arrived.append(along(messages[apart], "y", apart))
    grad_wv = (kept_val + swapped[0].astype(F32)).astype(BF16)
    grad_wo = (kept_out + swapped[1].astype(F32)).astype(BF16)
    arrived, grad_wv, grad_wo, grad_filter, grad_tail = lax.optimization_barrier(
        (arrived, grad_wv, grad_wo, grad_filter, grad_tail)
    )
    grad_local, gain_term = ended(place, arrived, x_rows, cot_rows, gain_row[None], inv_rms)
    received = along(grad_local, "section", -1)
    gain_term = with_partner(gain_term, "z", 1)
    grad_gain = with_partner(gain_term, "core", 1).reshape(1, width)
    return (
        received[None],
        grad_wv[None],
        grad_wo[None],
        grad_filter[None],
        grad_tail[None],
        grad_gain,
    )


def solution(mesh):
    sections = mesh.shape["section"]
    split = Mesh(mesh.devices.reshape(sections, Y, Z, CORE), ("section", *TENSOR))
    by_rows = P("section", TENSOR, None)
    by_columns = P("section", None, TENSOR)
    whole = P("section", None)

    return jax.shard_map(
        on_device,
        mesh=split,
        in_specs=(by_rows, by_rows, whole, by_rows, by_rows, by_columns, by_columns, P("section")),
        out_specs=(by_rows, by_rows, by_rows, by_columns, by_columns, whole),
        check_vma=False,
    )
```
